32 devices in a mesh: slide: 4 (over x, core), seq: 8 (over z, y).
Axes of the slice: x: 2, y: 2, z: 4, core: 2. Of those that a mesh axis runs over, the one named last changes fastest.
Arguments:
- tiles: bfloat16 [32768, 768], P(('slide', 'seq')), may hold values from -6 to 6
- route: int32 [32768], P(('slide', 'seq')), may hold values from 0 to 32767, as said below
- counts: int32 [4], replicated, may hold values from 2048 to 8192, as said below
- w_qkv: bfloat16 [768, 2304], replicated
- w_out: bfloat16 [768, 768], replicated, may hold values from -0.21875 to 0.21875
Outputs:
- mixed: bfloat16 [32768, 768], P(('slide', 'seq'))
The draws below stay inside these ranges and needn't reach their ends.
Inputs may be any that keep to these rules, and one draw needn't show every extreme that they name: `route`: every position of the 4 x 8192 sequences is named exactly once. The rows of one loader device (aligned blocks of 1024 rows) name either 16 or 48 positions in each aligned block of 1024 positions, and exactly 48 in some of them. `counts`: at least one slide is full.
All inputs are finite; a program needn't handle non-finite values.
Results may differ from the reference program's by a relative error of at most 0.0067.
Values may be sent and summed in bfloat16 or wider, within the bound.
A program may use at most 128 MiB of HBM per device.

```python
import jax
import jax.numpy as jnp
from jax import lax

D = 768
HEADS = 16
HEAD_DIM = 48
TOK_DEV = 1024
RATE_MID = 4
SLIDES = 4
CAP = 8192
LOADERS = 32
MOST = 48
N_SEQ = 8


def ranks_of(labels, owners):
    order = jnp.argsort(labels, stable=True)
    sorted_labels = labels[order]
    sizes = jnp.sum((labels[:, None] == jnp.arange(owners)[None, :]).astype(jnp.int32), 0)
    starts = jnp.cumsum(sizes) - sizes
    placed_rank = jnp.arange(labels.shape[0], dtype=jnp.int32) - starts[sorted_labels]
    return jnp.zeros_like(labels).at[order].set(placed_rank.astype(jnp.int32))


def draw_route(key, part):
    owners = LOADERS
    base = TOK_DEV // owners
    swing = base // 2
    key_roll, key_send, key_take = jax.random.split(jax.random.fold_in(key, 11), 3)
    roll = jax.random.randint(key_roll, (), 0, 2)
    index = jnp.arange(owners)
    parity = (index[None, :] - index[:, None] + roll) % 2
    amounts = base + swing * jnp.where(parity == 0, 1, -1)

    def labels_for(one_key, row):
        labels = jnp.repeat(index, row, total_repeat_length=TOK_DEV).astype(jnp.int32)
        return jax.random.permutation(one_key, labels)
    send_labels = jax.vmap(labels_for)(jax.random.split(key_send, owners), amounts)
    take_labels = jax.vmap(labels_for)(jax.random.split(key_take, owners), jnp.transpose(amounts))
    send_rank = jax.vmap(lambda labels: ranks_of(labels, owners))(send_labels)
    take_rank = jax.vmap(lambda labels: ranks_of(labels, owners))(take_labels)
    owner_index = jnp.broadcast_to(index[:, None], (owners, TOK_DEV))
    slot_index = jnp.broadcast_to(jnp.arange(TOK_DEV)[None, :], (owners, TOK_DEV))
    table = jnp.zeros((owners, owners, MOST), jnp.int32)
    table = table.at[owner_index, take_labels, take_rank].set(slot_index.astype(jnp.int32))
    source_index = jnp.broadcast_to(index[:, None], (owners, TOK_DEV))
    slots = table[send_labels, source_index, send_rank]
    return (send_labels * TOK_DEV + slots).reshape(owners * TOK_DEV).astype(jnp.int32)


def draw_counts(key, part):
    key_len, key_full = jax.random.split(jax.random.fold_in(key, 23))
    lengths = jax.random.randint(key_len, (SLIDES,), CAP // 4, CAP + 1)
    full = jax.random.randint(key_full, (), 0, SLIDES)
    return jnp.where(jnp.arange(SLIDES) == full, CAP, lengths).astype(jnp.int32)


def draw_w_qkv(key, part):
    key_base = jax.random.fold_in(jax.random.fold_in(key, 37), 0)
    base = jax.random.normal(key_base, (D, 3 * D), jnp.float32) * D ** (-0.5)
    return base.astype(jnp.bfloat16)


def block_scale(key, dims, cuts, smallest, largest):
    loudness = 1.0
    for position, shards_of in cuts:
        steps = jax.random.uniform(jax.random.fold_in(jax.random.fold_in(key, 6), position), (shards_of,), jnp.float32, smallest / len(cuts), largest / len(cuts))
        loudness = loudness * jnp.repeat(jnp.exp(steps), dims[position] // shards_of).reshape((-1,) + (1,) * (len(dims) - 1 - position))
    return loudness


def normal_values(own_key, dims, width, most, cuts=(), kind=jnp.bfloat16):
    values = jax.random.normal(own_key, dims, jnp.float32) * width
    if len(cuts) > 0:
        values = block_scale(own_key, dims, cuts, -0.22, 0.18) * values
    return jnp.clip(values, min=-most, max=most).astype(kind)


def setup_inputs(seed: int = 0) -> dict:
    seeds = jax.random.split(jax.random.key(seed), 6)
    tiles = normal_values(seeds[0], (SLIDES * CAP, D), 1.0, 6.0, ((0, 32),))
    route = draw_route(jax.random.fold_in(seeds[5], 71), 0)
    counts = draw_counts(jax.random.fold_in(seeds[5], 71), 0)
    w_qkv = draw_w_qkv(jax.random.fold_in(seeds[5], 71), 0)
    w_out = normal_values(seeds[4], (D, D), D ** -0.5, 0.21875)
    return {"tiles": tiles, "route": route, "counts": counts, "w_qkv": w_qkv, "w_out": w_out}


def layer_norm(values):
    mean = lax.optimization_barrier(jnp.mean(values, -1, keepdims=True))
    centred = values - mean
    var = lax.optimization_barrier(jnp.mean(centred * centred, -1, keepdims=True))
    return centred * lax.rsqrt(var + 1e-05)

def attend(query, keys, values, key_valid):
    scale = 1.0 / HEAD_DIM ** 0.5
    rows = query.shape[0]
    block = min(512, rows)
    keys_wide = keys.astype(jnp.float32)
    values_wide = values.astype(jnp.float32)
    mask = jnp.transpose(key_valid)[:, None, :]

    def one_block(query_block):
        scores = jnp.einsum('qhd,khd->hqk', query_block.astype(jnp.float32), keys_wide) * scale
        scores = jnp.where(mask, scores, -1e+30)
        top = lax.optimization_barrier(jnp.max(scores, -1))
        weights = jnp.where(mask, jnp.exp(scores - top[..., None]), 0.0)
        total = lax.optimization_barrier(jnp.sum(weights, -1))
        rounded = lax.optimization_barrier(weights.astype(jnp.bfloat16)).astype(jnp.float32)
        result = jnp.einsum('hqk,khd->qhd', rounded, values_wide)
        return (result, jnp.transpose(top), jnp.transpose(total))
    blocks = query.reshape(rows // block, block, HEADS, HEAD_DIM)
    result, top, total = lax.map(one_block, blocks)
    return (result.reshape(rows, HEADS, HEAD_DIM), top.reshape(rows, HEADS), total.reshape(rows, HEADS))

def picker(rate):
    return jnp.arange(HEADS)[None, :] % rate == jnp.arange(rate)[:, None]

def select(array, rate):
    pick = picker(rate).astype(array.dtype)
    shaped = array.reshape(array.shape[0] // rate, rate, HEADS, HEAD_DIM)
    return lax.optimization_barrier(jnp.sum(shaped * pick[None, :, :, None], 1)).astype(array.dtype)

def spread(result, top, total, rate):
    pick = picker(rate)
    count_rows = result.shape[0] * rate
    full = (result[:, None] * pick[None, :, :, None].astype(jnp.float32)).reshape(count_rows, HEADS, HEAD_DIM)
    top_full = jnp.where(pick[None], top[:, None, :], -1e+30).reshape(count_rows, HEADS)
    total_full = (total[:, None, :] * pick[None].astype(jnp.float32)).reshape(count_rows, HEADS)
    return (full, top_full, total_full)

def level(query, keys, values, count, segment, rate):
    taken = CAP // rate
    nseg = CAP // segment
    sub = segment // rate
    positions = jnp.arange(taken)[:, None] * rate + (jnp.arange(HEADS) % rate)[None, :]
    key_valid = positions < count
    pieces = (select(query, rate).reshape(nseg, sub, HEADS, HEAD_DIM), select(keys, rate).reshape(nseg, sub, HEADS, HEAD_DIM), select(values, rate).reshape(nseg, sub, HEADS, HEAD_DIM), key_valid.reshape(nseg, sub, HEADS))
    result, top, total = lax.map(lambda item: attend(item[0], item[1], item[2], item[3]), pieces)
    return spread(result.reshape(taken, HEADS, HEAD_DIM), top.reshape(taken, HEADS), total.reshape(taken, HEADS), rate)

def one_slide(item, w_qkv, w_out):
    placed, count = item
    valid = jnp.arange(CAP) < count
    normed = layer_norm(placed.astype(jnp.float32)).astype(jnp.bfloat16)
    qkv = jnp.dot(normed, w_qkv, preferred_element_type=jnp.float32).astype(jnp.bfloat16)
    qkv = qkv.reshape(CAP, 3, HEADS, HEAD_DIM)
    query, keys, values = (qkv[:, 0], qkv[:, 1], qkv[:, 2])
    levels = [level(query, keys, values, count, TOK_DEV // 2, 1), level(query, keys, values, count, RATE_MID * TOK_DEV, RATE_MID), level(query, keys, values, count, CAP, N_SEQ)]
    highest = jnp.maximum(jnp.maximum(levels[0][1], levels[1][1]), levels[2][1])
    numer = jnp.zeros((CAP, HEADS, HEAD_DIM), jnp.float32)
    denom = jnp.zeros((CAP, HEADS), jnp.float32)
    for result, top, total in levels:
        factor = jnp.exp(top - highest)
        numer = numer + factor[..., None] * result
        denom = denom + factor * total
    denom = jnp.where(valid[:, None], denom, 1.0)
    attended = jnp.where(valid[:, None, None], numer / denom[..., None], 0.0)
    attended = attended.reshape(CAP, D).astype(jnp.bfloat16)
    projected = jnp.dot(attended, w_out, preferred_element_type=jnp.float32)
    mixed = placed.astype(jnp.float32) + layer_norm(projected)
    return jnp.where(valid[:, None], mixed, 0.0).astype(jnp.bfloat16)

def reference(tiles, route, counts, w_qkv, w_out):
    placed = jnp.zeros((SLIDES * CAP, D), jnp.bfloat16).at[route].set(tiles)
    placed = placed.reshape(SLIDES, CAP, D)
    mixed = lax.map(lambda item: one_slide(item, w_qkv, w_out), (placed, counts))
    return mixed.reshape(SLIDES * CAP, D)
```

```python
import functools
import math

import jax
import jax.numpy as jnp
from jax import lax
from jax.experimental import pallas as pl
from jax.experimental.pallas import tpu as pltpu
from jax.sharding import PartitionSpec as P

HEADS = 16
GROUP = 4
LANES = 128
TAIL = 16
BF = jnp.bfloat16
F32 = jnp.float32
I32 = jnp.int32
MESH = pl.DeviceIdType.MESH


def iota(shape, dim):
    return lax.broadcasted_iota(I32, shape, dim)


def dot(a, b):
    return jnp.dot(a, b, preferred_element_type=F32)


def dot_nt(a, b):
    return lax.dot_general(a, b, (((1,), (1,)), ((), ())), preferred_element_type=F32)


def one_hot(condition):
    return jnp.where(condition, 1.0, 0.0).astype(BF)


def position_of(row, half, n_seq):
    run = half // n_seq
    block = (row % half) // run
    groups = n_seq // GROUP
    residue = (block % groups) * GROUP + block // groups
    return (row // half) * half + (row % run) * n_seq + residue


def row_of(position, half, n_seq):
    run = half // n_seq
    within = position % half
    residue = within % n_seq
    block = (residue % GROUP) * (n_seq // GROUP) + residue // GROUP
    return (position // half) * half + block * run + within // n_seq


def layer_norm(values, axis):
    mean = jnp.mean(values, axis, keepdims=True)
    centred = values - mean
    var = jnp.mean(centred * centred, axis, keepdims=True)
    return centred * lax.rsqrt(var + 1e-05)


def pieces(value):
    first = value.astype(BF).astype(F32)
    second = (value - first).astype(BF).astype(F32)
    return first, second, value - first - second


def soft_units(units):
    def score(unit):
        keys, query, head, _, _ = unit
        q = query()
        width = q.shape[1]
        zero = jnp.zeros(q.shape, BF)
        flag = one_hot(iota((32, width), 0) == 0)
        return dot(keys(), jnp.concatenate(([q, zero] if head == 0 else [zero, q]) + [flag], 0))

    def finish(unit, top, weights):
        values, sink = unit[3], unit[4]
        v = values()
        both = jnp.concatenate([v, jnp.ones((TAIL, v.shape[1]), BF)], 0)
        result = dot(both, weights)
        size = v.shape[0]
        total = result[size : size + 1]
        sink(result[:size] * (1.0 / total), top + jnp.log2(total))

    scores, held = score(units[0]), None
    for index, unit in enumerate(units):
        later = score(units[index + 1]) if index + 1 < len(units) else None
        top = jnp.max(scores, 0, keepdims=True)
        weights = jnp.exp2(scores - top).astype(BF)
        if held is not None:
            finish(*held)
        held, scores = (unit, top, weights), later
    finish(*held)


def layer_kernel(
    dims, counts_ref, route_ref, tiles_ref, w_qkv_ref, w_out_ref, out_ref,
    w_qkv, w_out, wq_t, wv_t, wk, wo_t, outgoing, arrived, meta_out, meta_in, placed,
    q_t, keys, v_t, att, near, near_log,
    mid_q, mid_k, mid_v, mid_out, mid_back, wide_qv, wide_k, wide_qv_in, wide_k_in, wide_out, wide_back,
    load_sem, d_send, d_recv, p_send, p_recv, mf_send, mf_recv, wf_send, wf_recv, mb_send, mb_recv,
    wb_send, wb_recv, own_sem,
):
    n_slide, n_seq, most, stride = dims
    owners = n_slide * n_seq
    rows, width = tiles_ref.shape
    half = rows // 2
    run = half // n_seq
    taken = 2 * run
    size = width // HEADS
    duo = 2 * size
    per_owner = width // GROUP
    factor = math.log2(math.e) / math.sqrt(size)
    slide, seq = lax.axis_index("slide"), lax.axis_index("seq")
    member = seq % GROUP
    base = seq - member

    def device_at(k):
        return ((slide + k // n_seq) % n_slide, (seq + k % n_seq) % n_seq)

    barrier = pltpu.get_barrier_semaphore()

    def greet(k, carry):
        pl.semaphore_signal(barrier, inc=1, device_id=device_at(k), device_id_type=MESH)
        return carry

    lax.fori_loop(1, owners, greet, 0)
    load_qkv = pltpu.make_async_copy(w_qkv_ref, w_qkv, load_sem.at[0])
    load_out = pltpu.make_async_copy(w_out_ref, w_out, load_sem.at[1])
    load_qkv.start()
    load_out.start()

    if stride > most:
        arrived[:, most:, :] = jnp.zeros((owners, stride - most, width), BF)
    route = route_ref[...]
    owner = route // rows
    offset = ((owner // n_seq - slide + n_slide) % n_slide) * n_seq
    offset = offset + (owner % n_seq - seq + n_seq) % n_seq
    mine = iota((owners, rows), 0) == offset
    upper = one_hot(iota((rows, rows), 0) <= iota((rows, rows), 1))
    counted = dot(one_hot(mine), upper)
    rank = jnp.sum(jnp.where(mine, counted, 0.0), 0, keepdims=True).astype(I32) - 1
    slot = offset * stride + rank
    local = row_of(route % rows, half, n_seq)
    kind = iota((16, rows), 0)
    digits = jnp.where(
        kind == 0, local // 32, jnp.where(kind == 1, local % 32, jnp.where(kind == 2, 1, 0))
    ).astype(F32).astype(BF)

    def dispatch_copy(k):
        return pltpu.make_async_remote_copy(
            src_ref=outgoing.at[k, pl.ds(0, most)], dst_ref=arrived.at[k, pl.ds(0, most)],
            send_sem=d_send.at[k], recv_sem=d_recv.at[k], device_id=device_at(k), device_id_type=MESH,
        )

    per_row = LANES // stride

    def place_copy(k):
        return pltpu.make_async_remote_copy(
            src_ref=meta_out.at[k // per_row], dst_ref=meta_in.at[k],
            send_sem=p_send.at[k], recv_sem=p_recv.at[k], device_id=device_at(k), device_id_type=MESH,
        )

    def start_dispatch(k, carry):
        place_copy(k).start()
        dispatch_copy(k).start()
        return carry

    chunk = 2 * LANES
    blocks = chunk // stride
    for c in range(owners // blocks):
        move = one_hot(iota((chunk, rows), 0) + c * chunk == slot)
        sent = dot_nt(digits, move)
        place = sent[0:1] * 32.0 + sent[1:2] + (1.0 - sent[2:3]) * (2.0 * rows)
        for i in range(2):
            meta_out[2 * c + i] = place[:, i * LANES : (i + 1) * LANES]
        moved = dot(move, tiles_ref[...]).astype(BF)
        outgoing[c * blocks : (c + 1) * blocks] = moved.reshape(blocks, stride, width)
        if c == 0:
            arrived[0] = moved[:stride]
            meta_in[0] = place[:, :LANES]
            pl.semaphore_wait(barrier, owners - 1)
        lax.fori_loop(max(1, c * blocks), (c + 1) * blocks, start_dispatch, 0)

    load_qkv.wait()
    load_out.wait()
    feature = iota((width, width), 0)
    inner = feature % per_owner
    head = feature // per_owner + GROUP * (inner // duo) + 2 * GROUP * ((inner % duo) // size)
    reorder = one_hot(head * size + inner % size == iota((width, width), 1))
    wq_t[...] = dot_nt(reorder, w_qkv[:, :width]).astype(BF)
    wv_t[...] = dot_nt(reorder, w_qkv[:, 2 * width :]).astype(BF)
    padded = HEADS // 2 * LANES
    column = iota((width, padded), 1)
    pair, lane = column // LANES, column % LANES
    source = (pair // 2 + GROUP * (pair % 2) + 2 * GROUP * (lane // size)) * size + lane % size
    pick = one_hot((iota((width, padded), 0) == source) & (lane < duo))
    wk[...] = dot(w_qkv[:, width : 2 * width], pick).astype(BF)
    unit_matrix = one_hot(iota((width, width), 0) == iota((width, width), 1))
    wo_t[...] = dot_nt(unit_matrix, dot(reorder, w_out[...]).astype(BF)).astype(BF)

    def wait_dispatch(k, carry):
        place_copy(k).wait_recv()
        dispatch_copy(k).wait_recv()
        return carry

    depth = 4 * LANES
    many = depth // stride
    for g in range(owners // many):
        lax.fori_loop(max(1, g * many), (g + 1) * many, wait_dispatch, 0)
        parts = []
        for i in range(g * depth // LANES, (g + 1) * depth // LANES):
            part = meta_in[i * per_row]
            for b in range(1, per_row):
                part = jnp.where(iota((1, LANES), 1) // stride == b, meta_in[i * per_row + b], part)
            parts.append(part)
        place = jnp.concatenate(parts, 1).astype(I32)
        take = one_hot(iota((rows, depth), 0) == place)
        block = arrived[g * many : (g + 1) * many].reshape(depth, width)
        added = dot(take, block).astype(BF)
        placed[...] = added if g == 0 else placed[...] + added

    limit = counts_ref[slide] - seq * rows
    for seg in range(2):
        normed = layer_norm(placed[seg * half : (seg + 1) * half].astype(F32), 1).astype(BF)
        q = (dot_nt(wq_t[...], normed) * factor).astype(BF)
        v = dot_nt(wv_t[...], normed).astype(BF)
        for cb in range(GROUP):
            q_t[cb, seg] = q[:, cb * LANES : (cb + 1) * LANES]
            v_t[cb, seg] = v[:, cb * LANES : (cb + 1) * LANES]
        at = iota((half, 2 * LANES), 0) + seg * half
        valid = position_of(at, half, n_seq) < limit
        lane = iota((half, 2 * LANES), 1) % LANES
        bias = jnp.where((lane == duo) & jnp.logical_not(valid), -1e30, 0.0)
        for o in range(GROUP):
            k = (dot(normed, wk[:, o * 2 * LANES : (o + 1) * 2 * LANES]) + bias).astype(BF)
            for j in range(2):
                keys[o, j, seg] = k[:, j * LANES : (j + 1) * LANES]

    for r in range(n_seq):
        o, j, g = r % GROUP, (r // GROUP) % 2, r // GROUP
        start = o * per_owner + j * duo
        for index, ref in enumerate((q_t, v_t)):
            wide_qv[r, index] = jnp.concatenate(
                [ref[o, seg, start : start + duo, g * run : (g + 1) * run] for seg in range(2)], 1
            )
        for seg in range(2):
            first = o * LANES + g * run
            wide_k[r, seg * run : (seg + 1) * run] = keys[o, j, seg, first : first + run]

    def seq_at(k):
        return (slide, (seq + k) % n_seq)

    def seq_back(k):
        return (slide, (seq - k + n_seq) % n_seq)

    def wide_copies(k):
        to = (seq + k) % n_seq
        return [
            pltpu.make_async_remote_copy(
                src_ref=src.at[to], dst_ref=dst.at[k], send_sem=wf_send.at[k, i], recv_sem=wf_recv.at[k, i],
                device_id=seq_at(k), device_id_type=MESH,
            )
            for i, (src, dst) in enumerate(((wide_qv, wide_qv_in), (wide_k, wide_k_in)))
        ]

    def mid_sources(o):
        part = pl.ds(pl.multiple_of(o * per_owner, per_owner), per_owner)
        return (
            (q_t.at[o, :, part, :], mid_q),
            (keys.at[o, :, :, pl.ds(pl.multiple_of(o * LANES, LANES), LANES), :], mid_k),
            (v_t.at[o, :, part, :], mid_v),
        )

    def mid_copies(k):
        to = (member + k) % GROUP
        return [
            pltpu.make_async_remote_copy(
                src_ref=src, dst_ref=dst.at[k], send_sem=mf_send.at[k, i], recv_sem=mf_recv.at[k, i],
                device_id=(slide, base + to), device_id_type=MESH,
            )
            for i, (src, dst) in enumerate(mid_sources(to))
        ]

    for k in range(1, n_seq):
        for copy in wide_copies(k):
            copy.start()
    for k in range(1, GROUP):
        for copy in mid_copies(k):
            copy.start()
    own = [
        pltpu.make_async_copy(wide_qv.at[seq], wide_qv_in.at[0], own_sem.at[0]),
        pltpu.make_async_copy(wide_k.at[seq], wide_k_in.at[0], own_sem.at[1]),
    ]
    own += [
        pltpu.make_async_copy(src, dst.at[0], own_sem.at[2 + i])
        for i, (src, dst) in enumerate(mid_sources(member))
    ]
    for copy in own:
        copy.start()

    def near_owner(o, carry):
        units = []
        for j in range(2):
            for seg in range(2):
                for t in range(2):
                    part = pl.ds(pl.multiple_of(o * per_owner + (j * duo + t * size), TAIL), size)

                    def wide_row(ref, seg=seg, part=part):
                        return jnp.concatenate([ref[cb, seg, part, :] for cb in range(GROUP)], 1)

                    def sink(result, log, j=j, seg=seg, t=t, part=part):
                        for cb in range(GROUP):
                            cut = slice(cb * LANES, (cb + 1) * LANES)
                            att[seg, cb, part, :] = result[:, cut].astype(BF)
                            near[o, j, seg, t, cb] = result[:, cut]
                            near_log[o, j, seg, t, cb] = log[:, cut]

                    units.append((
                        lambda j=j, seg=seg: keys[o, j, seg],
                        lambda wide_row=wide_row: wide_row(q_t),
                        t,
                        lambda wide_row=wide_row: wide_row(v_t),
                        sink,
                    ))
        soft_units(units)
        return carry

    lax.fori_loop(0, GROUP, near_owner, 0)

    def log_tile(logs, lanes):
        tile = jnp.zeros((TAIL, lanes), F32)
        where = iota((TAIL, lanes), 0)
        for index, piece in enumerate(pieces(logs[0]) + pieces(logs[1])):
            tile = jnp.where(where == index, piece, tile)
        return tile.astype(BF)

    for copy in own:
        copy.wait()
    for k in range(1, n_seq):
        for copy in wide_copies(k):
            copy.wait_recv()

    def wide_return(k):
        return pltpu.make_async_remote_copy(
            src_ref=wide_out.at[k], dst_ref=wide_back.at[seq], send_sem=wb_send.at[k], recv_sem=wb_recv.at[k],
            device_id=seq_back(k), device_id_type=MESH,
        )

    order = [k % n_seq for k in range(1, n_seq + 1)]
    count = n_seq // 2
    units = []
    for part in range(2):
        slots = order[part * count : (part + 1) * count]
        logs = []
        for t in range(2):
            cut = slice(t * size, (t + 1) * size)

            def sink(result, log, t=t, slots=slots, cut=cut, logs=logs):
                logs.append(log)
                for index, k in enumerate(slots):
                    lanes = slice(index * taken, (index + 1) * taken)
                    wide_out[k, cut] = result[:, lanes].astype(BF)
                    if t == 1:
                        wide_out[k, duo:] = log_tile([one[:, lanes] for one in logs], taken)
                        if k:
                            wide_return(k).start()

            units.append((
                lambda: wide_k_in[...].reshape(n_seq * taken, LANES),
                lambda slots=slots, cut=cut: jnp.concatenate([wide_qv_in[k, 0, cut] for k in slots], 1),
                t,
                lambda cut=cut: jnp.concatenate([wide_qv_in[k, 1, cut] for k in range(n_seq)], 1),
                sink,
            ))
    soft_units(units)
    own_wide = pltpu.make_async_copy(wide_out.at[0], wide_back.at[seq], own_sem.at[0])
    own_wide.start()

    for k in range(1, GROUP):
        for copy in mid_copies(k):
            copy.wait_recv()

    def mid_return(k):
        return pltpu.make_async_remote_copy(
            src_ref=mid_out.at[k], dst_ref=mid_back.at[member], send_sem=mb_send.at[k], recv_sem=mb_recv.at[k],
            device_id=(slide, base + (member - k + GROUP) % GROUP), device_id_type=MESH,
        )

    for slots in ((1, 2), (3, 0)):
        units = []
        for j in range(2):
            logs = []
            for t in range(2):
                cut = slice(j * duo + t * size, j * duo + (t + 1) * size)

                def sink(result, log, j=j, t=t, slots=slots, logs=logs):
                    logs.append(log)
                    for index, (k, seg) in enumerate((k, seg) for k in slots for seg in range(2)):
                        lanes = slice(index * LANES, (index + 1) * LANES)
                        mid_out[k, seg, j, t * size : (t + 1) * size] = result[:, lanes].astype(BF)
                        if t == 1:
                            mid_out[k, seg, j, duo:] = log_tile([one[:, lanes] for one in logs], LANES)

                units.append((
                    lambda j=j: mid_k[:, j].reshape(rows, LANES),
                    lambda slots=slots, cut=cut: jnp.concatenate(
                        [mid_q[k, seg, cut] for k in slots for seg in range(2)], 1
                    ),
                    t,
                    lambda cut=cut: jnp.concatenate(
                        [mid_v[k, seg, cut] for k in range(GROUP) for seg in range(2)], 1
                    ),
                    sink,
                ))
        soft_units(units)
        for k in slots:
            if k:
                mid_return(k).start()
    own_mid = pltpu.make_async_copy(mid_out.at[0], mid_back.at[member], own_sem.at[1])
    own_mid.start()

    own_wide.wait()
    own_mid.wait()
    for k in range(1, n_seq):
        wide_return(k).wait_recv()
    for k in range(1, GROUP):
        mid_return(k).wait_recv()

    def log_of(tile, t):
        return tile[3 * t : 3 * t + 1] + tile[3 * t + 1 : 3 * t + 2] + tile[3 * t + 2 : 3 * t + 3]

    def embed(value, g, fill):
        before = [jnp.full((value.shape[0], g * run), fill, F32)] if g else []
        after = LANES - (g + 1) * run
        behind = [jnp.full((value.shape[0], after), fill, F32)] if after else []
        return jnp.concatenate(before + [value] + behind, 1)

    for o in range(GROUP):
        for j in range(2):
            for t in range(2):
                residue = (o + GROUP * j + 2 * GROUP * t) % n_seq
                wide = wide_back[residue].astype(F32)
                cut = slice(t * size, (t + 1) * size)
                start = o * per_owner + j * duo + t * size
                for seg in range(2):
                    lanes = slice(seg * run, (seg + 1) * run)
                    wide_o = embed(wide[cut, lanes], residue // GROUP, 0.0)
                    log_w = embed(log_of(wide[duo:, lanes], t), residue // GROUP, -3e30)
                    mid = mid_back[o, seg, j].astype(F32)
                    log_m = log_of(mid[duo:], t)
                    log_n = near_log[o, j, seg, t, o]
                    top = jnp.maximum(jnp.maximum(log_n, log_m), log_w)
                    share_n, share_m, share_w = jnp.exp2(log_n - top), jnp.exp2(log_m - top), jnp.exp2(log_w - top)
                    scale = 1.0 / (share_n + share_m + share_w)
                    merged = (
                        near[o, j, seg, t, o] * (share_n * scale)
                        + mid[cut] * (share_m * scale)
                        + wide_o * (share_w * scale)
                    )
                    att[seg, o, start : start + size, :] = merged.astype(BF)

    unsort = one_hot(row_of(iota((half, half), 0), half, n_seq) == iota((half, half), 1))
    for seg in range(2):
        attended = jnp.concatenate([att[seg, cb] for cb in range(GROUP)], 1)
        normed = layer_norm(dot(wo_t[...], attended), 0).astype(BF)
        mixed = dot_nt(unsort, normed) + dot(unsort, placed[seg * half : (seg + 1) * half])
        position = iota((half, width), 0) + seg * half
        out_ref[seg * half : (seg + 1) * half] = jnp.where(position < limit, mixed, 0.0).astype(BF)

    def drain(k, carry):
        place_copy(k).wait_send()
        dispatch_copy(k).wait_send()
        return carry

    lax.fori_loop(1, owners, drain, 0)
    for k in range(1, n_seq):
        for copy in wide_copies(k):
            copy.wait_send()
        wide_return(k).wait_send()
    for k in range(1, GROUP):
        for copy in mid_copies(k):
            copy.wait_send()
        mid_return(k).wait_send()


def body(tiles, route, counts, w_qkv, w_out):
    rows, width = tiles.shape
    n_slide = lax.axis_size("slide")
    n_seq = lax.axis_size("seq")
    owners = n_slide * n_seq
    most = -(-(3 * rows // (2 * owners)) // 16) * 16
    stride = 1 << (most - 1).bit_length()
    half = rows // 2
    taken = rows // n_seq
    size = width // HEADS
    duo = 2 * size
    per_owner = width // GROUP
    back = duo + TAIL
    vmem = pl.BlockSpec(memory_space=pltpu.VMEM)
    dma = pltpu.SemaphoreType.DMA

    def buffer(*shape, dtype=BF):
        return pltpu.VMEM(shape, dtype)

    return pl.pallas_call(
        functools.partial(layer_kernel, (n_slide, n_seq, most, stride)),
        out_shape=jax.ShapeDtypeStruct((rows, width), BF),
        in_specs=[
            pl.BlockSpec(memory_space=pltpu.SMEM), vmem, vmem,
            pl.BlockSpec(memory_space=pl.ANY), pl.BlockSpec(memory_space=pl.ANY),
        ],
        out_specs=vmem,
        scratch_shapes=[
            buffer(width, 3 * width),
            buffer(width, width),
            buffer(width, width),
            buffer(width, width),
            buffer(width, HEADS // 2 * LANES),
            buffer(width, width),
            buffer(owners, stride, width),
            buffer(owners, stride, width),
            buffer(owners * stride // LANES, 1, LANES, dtype=F32),
            buffer(owners, 1, LANES, dtype=F32),
            buffer(rows, width),
            buffer(GROUP, 2, width, LANES),
            buffer(GROUP, 2, 2, half, LANES),
            buffer(GROUP, 2, width, LANES),
            buffer(2, GROUP, width, LANES),
            buffer(GROUP, 2, 2, 2, GROUP, size, LANES, dtype=F32),
            buffer(GROUP, 2, 2, 2, GROUP, 1, LANES, dtype=F32),
            buffer(GROUP, 2, per_owner, LANES),
            buffer(GROUP, 2, 2, LANES, LANES),
            buffer(GROUP, 2, per_owner, LANES),
            buffer(GROUP, 2, 2, back, LANES),
            buffer(GROUP, 2, 2, back, LANES),
            buffer(n_seq, 2, duo, taken),
            buffer(n_seq, taken, LANES),
            buffer(n_seq, 2, duo, taken),
            buffer(n_seq, taken, LANES),
            buffer(n_seq, back, taken),
            buffer(n_seq, back, taken),
            dma((2,)),
            dma((owners,)), dma((owners,)), dma((owners,)), dma((owners,)),
            dma((GROUP, 3)), dma((GROUP, 3)), dma((n_seq, 2)), dma((n_seq, 2)),
            dma((GROUP,)), dma((GROUP,)), dma((n_seq,)), dma((n_seq,)),
            dma((5,)),
        ],
        compiler_params=pltpu.CompilerParams(
            collective_id=0, has_side_effects=True, vmem_limit_bytes=56 << 20
        ),
        name="layer",
    )(counts, route.reshape(1, rows), tiles, w_qkv, w_out)


def solution(mesh):
    return jax.shard_map(
        body,
        mesh=mesh,
        in_specs=(P(("slide", "seq"), None), P(("slide", "seq")), P(), P(), P()),
        out_specs=P(("slide", "seq"), None),
        check_vma=False,
    )
```

```python
import functools
import math

import jax
import jax.numpy as jnp
from jax import lax
from jax.experimental import pallas as pl
from jax.experimental.pallas import tpu as pltpu
from jax.sharding import PartitionSpec as P

HEADS = 16
GROUP = 4
LANES = 128
TAIL = 16
BF = jnp.bfloat16
F32 = jnp.float32
I32 = jnp.int32
MESH = pl.DeviceIdType.MESH


def iota(shape, dim):
    return lax.broadcasted_iota(I32, shape, dim)


def dot(a, b):
    return jnp.dot(a, b, preferred_element_type=F32)


def dot_nt(a, b):
    return lax.dot_general(a, b, (((1,), (1,)), ((), ())), preferred_element_type=F32)


def one_hot(condition):
    return jnp.where(condition, 1.0, 0.0).astype(BF)


def position_of(row, half, n_seq):
    run = half // n_seq
    block = (row % half) // run
    groups = n_seq // GROUP
    residue = (block % groups) * GROUP + block // groups
    return (row // half) * half + (row % run) * n_seq + residue


def row_of(position, half, n_seq):
    run = half // n_seq
    within = position % half
    residue = within % n_seq
    block = (residue % GROUP) * (n_seq // GROUP) + residue // GROUP
    return (position // half) * half + block * run + within // n_seq


def layer_norm(values, axis):
    mean = jnp.mean(values, axis, keepdims=True)
    centred = values - mean
    var = jnp.mean(centred * centred, axis, keepdims=True)
    return centred * lax.rsqrt(var + 1e-05)


def pieces(value):
    first = value.astype(BF).astype(F32)
    second = (value - first).astype(BF).astype(F32)
    return first, second, value - first - second


def soft_units(units):
    def score(unit):
        keys, query, head, _, _ = unit
        q = query()
        width = q.shape[1]
        zero = jnp.zeros(q.shape, BF)
        flag = one_hot(iota((32, width), 0) == 0)
        return dot(keys(), jnp.concatenate(([q, zero] if head == 0 else [zero, q]) + [flag], 0))

    def finish(unit, top, weights):
        values, sink = unit[3], unit[4]
        v = values()
        both = jnp.concatenate([v, jnp.ones((TAIL, v.shape[1]), BF)], 0)
        result = dot(both, weights)
        size = v.shape[0]
        total = result[size : size + 1]
        sink(result[:size] * (1.0 / total), top + jnp.log2(total))

    scores, held = score(units[0]), None
    for index, unit in enumerate(units):
        later = score(units[index + 1]) if index + 1 < len(units) else None
        top = jnp.max(scores, 0, keepdims=True)
        weights = jnp.exp2(scores - top).astype(BF)
        if held is not None:
            finish(*held)
        held, scores = (unit, top, weights), later
    finish(*held)


def layer_kernel(
    dims, counts_hbm, route_hbm, tiles_hbm, w_qkv_ref, w_out_ref, out_ref,
    counts_ref, route_ref, tiles_ref, placed, normed_ref, w_qkv, w_out, wq_t, wv_t, wk, wo_t, outgoing, arrived, meta_out, meta_in,
    q_t, keys, v_t, att, near, near_log,
    mid_q, mid_k, mid_v, mid_out, mid_back, wide_qv, wide_k, wide_qv_in, wide_k_in, wide_out, wide_back,
    load_sem, d_send, d_recv, p_send, p_recv, mf_send, mf_recv, wf_send, wf_recv, mb_send, mb_recv,
    wb_send, wb_recv, own_sem,
):
    n_slide, n_seq, most, stride = dims
    owners = n_slide * n_seq
    rows, width = tiles_ref.shape
    half = rows // 2
    run = half // n_seq
    taken = 2 * run
    size = width // HEADS
    duo = 2 * size
    middle_width = width // 2
    factor = math.log2(math.e) / math.sqrt(size)
    slide, seq = lax.axis_index("slide"), lax.axis_index("seq")
    member = seq % GROUP
    group = seq // GROUP
    groups = n_seq // GROUP
    base = seq - member

    def device_at(k):
        return ((slide + k // n_seq) % n_slide, (seq + k % n_seq) % n_seq)

    barrier = pltpu.get_barrier_semaphore()

    def greet(k, carry):
        pl.semaphore_signal(barrier, inc=1, device_id=device_at(k), device_id_type=MESH)
        return carry

    lax.fori_loop(1, owners, greet, 0)
    load_route = pltpu.make_async_copy(route_hbm, route_ref, load_sem.at[2])
    load_tiles = pltpu.make_async_copy(tiles_hbm, tiles_ref, load_sem.at[3])
    load_counts = pltpu.make_async_copy(counts_hbm, counts_ref, load_sem.at[4])
    load_route.start()
    load_tiles.start()
    load_counts.start()
    load_qkv = pltpu.make_async_copy(w_qkv_ref, w_qkv, load_sem.at[0])
    load_out = pltpu.make_async_copy(w_out_ref, w_out, load_sem.at[1])
    load_qkv.start()
    load_out.start()

    if stride > most:
        arrived[:, most:, :] = jnp.zeros((owners, stride - most, width), BF)
    upper = one_hot(iota((rows, rows), 0) <= iota((rows, rows), 1))
    load_route.wait()
    route = route_ref[...]
    owner = route // rows
    offset = ((owner // n_seq - slide + n_slide) % n_slide) * n_seq
    offset = offset + (owner % n_seq - seq + n_seq) % n_seq
    mine = iota((owners, rows), 0) == offset
    counted = dot(one_hot(mine), upper)
    rank = jnp.sum(jnp.where(mine, counted, 0.0), 0, keepdims=True).astype(I32) - 1
    slot = offset * stride + rank
    local = row_of(route % rows, half, n_seq)
    kind = iota((16, rows), 0)
    digits = jnp.where(
        kind == 0, local // 32, jnp.where(kind == 1, local % 32, jnp.where(kind == 2, 1, 0))
    ).astype(F32).astype(BF)

    def dispatch_copy(k):
        return pltpu.make_async_remote_copy(
            src_ref=outgoing.at[k, pl.ds(0, most)], dst_ref=arrived.at[k, pl.ds(0, most)],
            send_sem=d_send.at[k], recv_sem=d_recv.at[k], device_id=device_at(k), device_id_type=MESH,
        )

    per_row = LANES // stride

    def place_copy(k):
        return pltpu.make_async_remote_copy(
            src_ref=meta_out.at[k // per_row], dst_ref=meta_in.at[k],
            send_sem=p_send.at[k], recv_sem=p_recv.at[k], device_id=device_at(k), device_id_type=MESH,
        )

    def start_dispatch(k, carry):
        place_copy(k).start()
        dispatch_copy(k).start()
        return carry

    load_tiles.wait()
    load_counts.wait()
    chunk = 2 * LANES
    blocks = chunk // stride
    for c in range(owners // blocks):
        move = one_hot(iota((chunk, rows), 0) + c * chunk == slot)
        sent = dot_nt(digits, move)
        place = sent[0:1] * 32.0 + sent[1:2] + (1.0 - sent[2:3]) * (2.0 * rows)
        for i in range(2):
            meta_out[2 * c + i] = place[:, i * LANES : (i + 1) * LANES]
        moved = dot(move, tiles_ref[...]).astype(BF)
        outgoing[c * blocks : (c + 1) * blocks] = moved.reshape(blocks, stride, width)
        if c == 0:
            arrived[0] = moved[:stride]
            meta_in[0] = place[:, :LANES]
            pl.semaphore_wait(barrier, owners - 1)
        lax.fori_loop(max(1, c * blocks), (c + 1) * blocks, start_dispatch, 0)

    load_qkv.wait()
    load_out.wait()
    feature = iota((width, width), 0)
    head = (feature % middle_width) // duo + GROUP * (feature // middle_width) + 2 * GROUP * ((feature % duo) // size)
    reorder = one_hot(head * size + feature % size == iota((width, width), 1))
    wq_t[...] = dot_nt(reorder, w_qkv[:, :width]).astype(BF)
    wv_t[...] = dot_nt(reorder, w_qkv[:, 2 * width :]).astype(BF)
    padded = HEADS // 2 * LANES
    column = iota((width, padded), 1)
    pair, lane = column // LANES, column % LANES
    source = (pair + 2 * GROUP * (lane // size)) * size + lane % size
    pick = one_hot((iota((width, padded), 0) == source) & (lane < duo))
    wk[...] = dot(w_qkv[:, width : 2 * width], pick).astype(BF)
    unit_matrix = one_hot(iota((width, width), 0) == iota((width, width), 1))
    wo_t[...] = dot_nt(unit_matrix, dot(reorder, w_out[...]).astype(BF)).astype(BF)

    def wait_dispatch(k, carry):
        place_copy(k).wait_recv()
        dispatch_copy(k).wait_recv()
        return carry

    def places(first, last):
        parts = []
        for i in range(first * chunk // LANES, last * chunk // LANES):
            part = meta_in[i * per_row]
            for b in range(1, per_row):
                part = jnp.where(iota((1, LANES), 1) // stride == b, meta_in[i * per_row + b], part)
            parts.append(part)
        return jnp.concatenate(parts, 1).astype(I32)

    def arrivals(first, last):
        return arrived[first * blocks : last * blocks].reshape((last - first) * chunk, width)

    def spread(place, block):
        return dot(one_hot(iota((rows, place.shape[1]), 0) == place), block).astype(BF)

    def place_rows(first, last):
        added = spread(position_of(places(first, last), half, n_seq), arrivals(first, last))
        placed[...] = added if first == 0 else placed[...] + added

    steps = owners // blocks
    cuts = list(range(0, steps - 1, 2)) + [steps - 1, steps]
    for first, last in zip(cuts, cuts[1:]):
        lax.fori_loop(max(1, first * blocks), last * blocks, wait_dispatch, 0)
        added = spread(places(first, last), layer_norm(arrivals(first, last).astype(F32), 1).astype(BF))
        normed_ref[...] = added if first == 0 else normed_ref[...] + added
        if last < steps - 1:
            place_rows(first, last)

    limit = counts_ref[slide] - seq * rows

    def pair_at(turn):
        return (group + turn) % 2

    def project(turn):
        j = pair_at(turn)
        part = pl.ds(pl.multiple_of(j * middle_width, middle_width), middle_width)
        columns = pl.ds(pl.multiple_of(j * GROUP * LANES, GROUP * LANES), GROUP * LANES)
        for seg in range(2):
            normed = normed_ref[seg * half : (seg + 1) * half]
            q = (dot_nt(wq_t[part, :], normed) * factor).astype(BF)
            v = dot_nt(wv_t[part, :], normed).astype(BF)
            for cb in range(GROUP):
                q_t[cb, seg, part, :] = q[:, cb * LANES : (cb + 1) * LANES]
                v_t[cb, seg, part, :] = v[:, cb * LANES : (cb + 1) * LANES]
            at = iota((half, GROUP * LANES), 0) + seg * half
            valid = position_of(at, half, n_seq) < limit
            lane = iota((half, GROUP * LANES), 1) % LANES
            bias = jnp.where((lane == duo) & jnp.logical_not(valid), -1e30, 0.0)
            k = (dot(normed, wk[:, columns]) + bias).astype(BF)
            for o in range(GROUP):
                keys[j, o, seg] = k[:, o * LANES : (o + 1) * LANES]

    def mid_sources(o, j):
        part = pl.ds(pl.multiple_of(j * middle_width + o * duo, duo), duo)
        return (
            q_t.at[o, :, part, :],
            keys.at[j, o, :, pl.ds(pl.multiple_of(o * LANES, LANES), LANES), :],
            v_t.at[o, :, part, :],
        )

    def mid_copies(k, turn):
        to = (member + k) % GROUP
        return [
            pltpu.make_async_remote_copy(
                src_ref=src, dst_ref=dst.at[turn, k], send_sem=mf_send.at[turn, k, i],
                recv_sem=mf_recv.at[turn, k, i], device_id=(slide, base + to), device_id_type=MESH,
            )
            for i, (src, dst) in enumerate(zip(mid_sources(to, pair_at(turn)), (mid_q, mid_k, mid_v)))
        ]

    def start_mid(turn):
        for k in range(1, GROUP):
            for copy in mid_copies(k, turn):
                copy.start()

    project(0)
    start_mid(0)
    project(1)

    for r in range(n_seq):
        o, j, g = r % GROUP, (r // GROUP) % 2, r // GROUP
        start = j * middle_width + o * duo
        for index, ref in enumerate((q_t, v_t)):
            wide_qv[r, index] = jnp.concatenate(
                [ref[o, seg, start : start + duo, g * run : (g + 1) * run] for seg in range(2)], 1
            )
        for seg in range(2):
            first = o * LANES + g * run
            wide_k[r, seg * run : (seg + 1) * run] = keys[j, o, seg, first : first + run]

    def seq_at(k):
        return (group + k // GROUP) % groups * GROUP + (member + k % GROUP) % GROUP

    def seq_back(k):
        return (group - k // GROUP + groups) % groups * GROUP + (member - k % GROUP + GROUP) % GROUP

    def wide_copies(k):
        to = seq_at(k)
        return [
            pltpu.make_async_remote_copy(
                src_ref=src.at[to], dst_ref=dst.at[k], send_sem=wf_send.at[k, i], recv_sem=wf_recv.at[k, i],
                device_id=(slide, to), device_id_type=MESH,
            )
            for i, (src, dst) in enumerate(((wide_qv, wide_qv_in), (wide_k, wide_k_in)))
        ]

    for k in range(GROUP, n_seq):
        for copy in wide_copies(k):
            copy.start()
    own = [
        pltpu.make_async_copy(src, dst.at[turn, 0], own_sem.at[2 + 3 * turn + i])
        for turn in range(2)
        for i, (src, dst) in enumerate(zip(mid_sources(member, pair_at(turn)), (mid_q, mid_k, mid_v)))
    ]
    for copy in own:
        copy.start()

    def near_owner(o, carry):
        units = []
        for j in range(2):
            for seg in range(2):
                for t in range(2):
                    part = pl.ds(pl.multiple_of(o * duo + (j * middle_width + t * size), TAIL), size)

                    def wide_row(ref, seg=seg, part=part):
                        return jnp.concatenate([ref[cb, seg, part, :] for cb in range(GROUP)], 1)

                    def sink(result, log, j=j, seg=seg, t=t, part=part):
                        for cb in range(GROUP):
                            cut = slice(cb * LANES, (cb + 1) * LANES)
                            att[seg, cb, part, :] = result[:, cut].astype(BF)
                            near[o, j, seg, t, cb] = result[:, cut]
                            near_log[o, j, seg, t, cb] = log[:, cut]

                    units.append((
                        lambda j=j, seg=seg: keys[j, o, seg],
                        lambda wide_row=wide_row: wide_row(q_t),
                        t,
                        lambda wide_row=wide_row: wide_row(v_t),
                        sink,
                    ))
        soft_units(units)
        return carry

    lax.fori_loop(0, 2, near_owner, 0)
    start_mid(1)
    lax.fori_loop(2, GROUP, near_owner, 0)
    place_rows(cuts[-3], steps)

    def log_tile(logs, lanes):
        tile = jnp.zeros((TAIL, lanes), F32)
        where = iota((TAIL, lanes), 0)
        for index, piece in enumerate(pieces(logs[0]) + pieces(logs[1])):
            tile = jnp.where(where == index, piece, tile)
        return tile.astype(BF)

    for copy in own:
        copy.wait()

    def mid_return(k, turn):
        return pltpu.make_async_remote_copy(
            src_ref=mid_out.at[turn, k], dst_ref=mid_back.at[member, pair_at(turn)],
            send_sem=mb_send.at[turn, k], recv_sem=mb_recv.at[turn, k],
            device_id=(slide, base + (member - k + GROUP) % GROUP), device_id_type=MESH,
        )

    def wide_return(k):
        return pltpu.make_async_remote_copy(
            src_ref=wide_out.at[k], dst_ref=wide_back.at[seq], send_sem=wb_send.at[k], recv_sem=wb_recv.at[k],
            device_id=(slide, seq_back(k)), device_id_type=MESH,
        )

    def middle(turn):
        units = []
        for slots in ((1, 2), (3, 0)):
            logs = []
            for t in range(2):
                cut = slice(t * size, (t + 1) * size)

                def sink(result, log, t=t, cut=cut, slots=slots, logs=logs):
                    logs.append(log)
                    for index, (k, seg) in enumerate((k, seg) for k in slots for seg in range(2)):
                        lanes = slice(index * LANES, (index + 1) * LANES)
                        mid_out[turn, k, seg, cut] = result[:, lanes].astype(BF)
                        if t == 1:
                            mid_out[turn, k, seg, duo:] = log_tile([one[:, lanes] for one in logs], LANES)
                    if t == 1:
                        for k in slots:
                            if k:
                                mid_return(k, turn).start()

                units.append((
                    lambda: mid_k[turn].reshape(rows, LANES),
                    lambda slots=slots, cut=cut: jnp.concatenate(
                        [mid_q[turn, k, seg, cut] for k in slots for seg in range(2)], 1
                    ),
                    t,
                    lambda cut=cut: jnp.concatenate(
                        [mid_v[turn, k, seg, cut] for k in range(GROUP) for seg in range(2)], 1
                    ),
                    sink,
                ))
        return units

    def widest():
        order = [k % n_seq for k in range(1, n_seq + 1)]
        count = n_seq // 2
        units = []
        for part in range(2):
            slots = order[part * count : (part + 1) * count]
            logs = []
            for t in range(2):
                cut = slice(t * size, (t + 1) * size)

                def sink(result, log, t=t, slots=slots, cut=cut, logs=logs):
                    logs.append(log)
                    for index, k in enumerate(slots):
                        lanes = slice(index * taken, (index + 1) * taken)
                        wide_out[k, cut] = result[:, lanes].astype(BF)
                        if t == 1:
                            wide_out[k, duo:] = log_tile([one[:, lanes] for one in logs], taken)
                            if k:
                                wide_return(k).start()

                units.append((
                    lambda: wide_k_in[...].reshape(n_seq * taken, LANES),
                    lambda slots=slots, cut=cut: jnp.concatenate([wide_qv_in[k, 0, cut] for k in slots], 1),
                    t,
                    lambda cut=cut: jnp.concatenate([wide_qv_in[k, 1, cut] for k in range(n_seq)], 1),
                    sink,
                ))
        return units

    for k in range(1, GROUP):
        for copy in mid_copies(k, 0):
            copy.wait_recv()
    for k in range(GROUP):
        for index, ref in enumerate((mid_q, mid_v)):
            first, second = ref[0, k, 0], ref[0, k, 1]
            own_part = None
            for g in range(groups):
                lanes = slice(g * run, (g + 1) * run)
                part = jnp.concatenate([first[:, lanes], second[:, lanes]], 1)
                own_part = part if g == 0 else jnp.where(group == g, part, own_part)
            wide_qv_in[k, index] = own_part
        for seg in range(2):
            wide_k_in[k, seg * run : (seg + 1) * run] = mid_k[0, k, seg, pl.ds(pl.multiple_of(group * run, run), run)]
    soft_units(middle(0))
    for k in range(GROUP, n_seq):
        for copy in wide_copies(k):
            copy.wait_recv()
    soft_units(widest())
    own_wide = pltpu.make_async_copy(wide_out.at[0], wide_back.at[seq], own_sem.at[0])
    own_wide.start()
    for k in range(1, GROUP):
        for copy in mid_copies(k, 1):
            copy.wait_recv()
    soft_units(middle(1))
    own_mid = [
        pltpu.make_async_copy(mid_out.at[turn, 0], mid_back.at[member, pair_at(turn)], own_sem.at[1 + turn])
        for turn in range(2)
    ]
    for copy in own_mid:
        copy.start()

    own_wide.wait()
    for copy in own_mid:
        copy.wait()
    for k in range(1, n_seq):
        wide_return(k).wait_recv()
    for k in range(1, GROUP):
        for turn in range(2):
            mid_return(k, turn).wait_recv()

    def log_of(tile, t):
        return tile[3 * t : 3 * t + 1] + tile[3 * t + 1 : 3 * t + 2] + tile[3 * t + 2 : 3 * t + 3]

    def embed(value, g, fill):
        before = [jnp.full((value.shape[0], g * run), fill, F32)] if g else []
        after = LANES - (g + 1) * run
        behind = [jnp.full((value.shape[0], after), fill, F32)] if after else []
        return jnp.concatenate(before + [value] + behind, 1)

    for o in range(GROUP):
        for j in range(2):
            for t in range(2):
                residue = (o + GROUP * j + 2 * GROUP * t) % n_seq
                wide = wide_back[residue].astype(F32)
                cut = slice(t * size, (t + 1) * size)
                start = j * middle_width + o * duo + t * size
                for seg in range(2):
                    lanes = slice(seg * run, (seg + 1) * run)
                    wide_o = embed(wide[cut, lanes], residue // GROUP, 0.0)
                    log_w = embed(log_of(wide[duo:, lanes], t), residue // GROUP, -3e30)
                    mid = mid_back[o, j, seg].astype(F32)
                    log_m = log_of(mid[duo:], t)
                    log_n = near_log[o, j, seg, t, o]
                    top = jnp.maximum(jnp.maximum(log_n, log_m), log_w)
                    share_n, share_m, share_w = jnp.exp2(log_n - top), jnp.exp2(log_m - top), jnp.exp2(log_w - top)
                    scale = 1.0 / (share_n + share_m + share_w)
                    merged = (
                        near[o, j, seg, t, o] * (share_n * scale)
                        + mid[cut] * (share_m * scale)
                        + wide_o * (share_w * scale)
                    )
                    att[seg, o, start : start + size, :] = merged.astype(BF)

    unsort = one_hot(row_of(iota((half, half), 0), half, n_seq) == iota((half, half), 1))
    stores = []
    for seg in range(2):
        part = pl.ds(seg * half, half)
        attended = jnp.concatenate([att[seg, cb] for cb in range(GROUP)], 1)
        normed = layer_norm(dot(wo_t[...], attended), 0).astype(BF)
        value = dot_nt(unsort, normed) + placed[part, :].astype(F32)
        position = iota((half, width), 0) + seg * half
        tiles_ref[part, :] = jnp.where(position < limit, value, 0.0).astype(BF)
        stores.append(pltpu.make_async_copy(tiles_ref.at[part], out_ref.at[part], load_sem.at[seg]))
        stores[-1].start()

    def drain(k, carry):
        place_copy(k).wait_send()
        dispatch_copy(k).wait_send()
        return carry

    lax.fori_loop(1, owners, drain, 0)
    for k in range(1, n_seq):
        if k >= GROUP:
            for copy in wide_copies(k):
                copy.wait_send()
        wide_return(k).wait_send()
    for k in range(1, GROUP):
        for turn in range(2):
            for copy in mid_copies(k, turn):
                copy.wait_send()
            mid_return(k, turn).wait_send()
    for copy in stores:
        copy.wait()


def body(tiles, route, counts, w_qkv, w_out):
    rows, width = tiles.shape
    n_slide = lax.axis_size("slide")
    n_seq = lax.axis_size("seq")
    owners = n_slide * n_seq
    most = -(-(3 * rows // (2 * owners)) // 16) * 16
    stride = 1 << (most - 1).bit_length()
    half = rows // 2
    taken = rows // n_seq
    size = width // HEADS
    duo = 2 * size
    back = duo + TAIL
    dma = pltpu.SemaphoreType.DMA

    def buffer(*shape, dtype=BF):
        return pltpu.VMEM(shape, dtype)

    return pl.pallas_call(
        functools.partial(layer_kernel, (n_slide, n_seq, most, stride)),
        out_shape=jax.ShapeDtypeStruct((rows, width), BF),
        in_specs=[
            pl.BlockSpec(memory_space=pl.ANY),
        ] * 5,
        out_specs=pl.BlockSpec(memory_space=pl.ANY),
        scratch_shapes=[
            pltpu.SMEM((n_slide,), I32),
            buffer(1, rows, dtype=I32),
            buffer(rows, width),
            buffer(rows, width),
            buffer(rows, width),
            buffer(width, 3 * width),
            buffer(width, width),
            buffer(width, width),
            buffer(width, width),
            buffer(width, HEADS // 2 * LANES),
            buffer(width, width),
            buffer(owners, stride, width),
            buffer(owners, stride, width),
            buffer(owners * stride // LANES, 1, LANES, dtype=F32),
            buffer(owners, 1, LANES, dtype=F32),
            buffer(GROUP, 2, width, LANES),
            buffer(2, GROUP, 2, half, LANES),
            buffer(GROUP, 2, width, LANES),
            buffer(2, GROUP, width, LANES),
            buffer(GROUP, 2, 2, 2, GROUP, size, LANES, dtype=F32),
            buffer(GROUP, 2, 2, 2, GROUP, 1, LANES, dtype=F32),
            buffer(2, GROUP, 2, duo, LANES),
            buffer(2, GROUP, 2, LANES, LANES),
            buffer(2, GROUP, 2, duo, LANES),
            buffer(2, GROUP, 2, back, LANES),
            buffer(GROUP, 2, 2, back, LANES),
            buffer(n_seq, 2, duo, taken),
            buffer(n_seq, taken, LANES),
            buffer(n_seq, 2, duo, taken),
            buffer(n_seq, taken, LANES),
            buffer(n_seq, back, taken),
            buffer(n_seq, back, taken),
            dma((5,)),
            dma((owners,)), dma((owners,)), dma((owners,)), dma((owners,)),
            dma((2, GROUP, 3)), dma((2, GROUP, 3)), dma((n_seq, 2)), dma((n_seq, 2)),
            dma((2, GROUP)), dma((2, GROUP)), dma((n_seq,)), dma((n_seq,)),
            dma((8,)),
        ],
        compiler_params=pltpu.CompilerParams(
            collective_id=0, has_side_effects=True, vmem_limit_bytes=58 << 20
        ),
        name="layer",
    )(counts, route.reshape(1, rows), tiles, w_qkv, w_out)


def solution(mesh):
    return jax.shard_map(
        body,
        mesh=mesh,
        in_specs=(P(("slide", "seq"), None), P(("slide", "seq")), P(), P(), P()),
        out_specs=P(("slide", "seq"), None),
        check_vma=False,
    )
```

```python
import functools
import math

import jax
import jax.numpy as jnp
from jax import lax
from jax.experimental import pallas as pl
from jax.experimental.pallas import tpu as pltpu
from jax.sharding import PartitionSpec as P

HEADS = 16
GROUP = 4
LANES = 128
TAIL = 16
BF = jnp.bfloat16
F32 = jnp.float32
I32 = jnp.int32
MESH = pl.DeviceIdType.MESH


def iota(shape, dim):
    return lax.broadcasted_iota(I32, shape, dim)


def dot(a, b):
    return jnp.dot(a, b, preferred_element_type=F32)


def dot_nt(a, b):
    return lax.dot_general(a, b, (((1,), (1,)), ((), ())), preferred_element_type=F32)


def one_hot(condition):
    return jnp.where(condition, 1.0, 0.0).astype(BF)


def position_of(row, half, n_seq):
    run = half // n_seq
    block = (row % half) // run
    groups = n_seq // GROUP
    residue = (block % groups) * GROUP + block // groups
    return (row // half) * half + (row % run) * n_seq + residue


def row_of(position, half, n_seq):
    run = half // n_seq
    within = position % half
    residue = within % n_seq
    block = (residue % GROUP) * (n_seq // GROUP) + residue // GROUP
    return (position // half) * half + block * run + within // n_seq


def layer_norm(values, axis):
    mean = jnp.mean(values, axis, keepdims=True)
    centred = values - mean
    var = jnp.mean(centred * centred, axis, keepdims=True)
    return centred * lax.rsqrt(var + 1e-05)


def pieces(value):
    first = value.astype(BF).astype(F32)
    second = (value - first).astype(BF).astype(F32)
    return first, second, value - first - second


def soft_units(units):
    def score(unit):
        keys, query, head, _, _ = unit
        q = query()
        width = q.shape[1]
        zero = jnp.zeros(q.shape, BF)
        flag = one_hot(iota((32, width), 0) == 0)
        return dot(keys(), jnp.concatenate(([q, zero] if head == 0 else [zero, q]) + [flag], 0))

    def finish(unit, top, weights):
        values, sink = unit[3], unit[4]
        v = values()
        both = jnp.concatenate([v, jnp.ones((TAIL, v.shape[1]), BF)], 0)
        result = dot(both, weights)
        size = v.shape[0]
        total = result[size : size + 1]
        sink(result[:size] * (1.0 / total), top + jnp.log2(total))

    scores, held = score(units[0]), None
    for index, unit in enumerate(units):
        later = score(units[index + 1]) if index + 1 < len(units) else None
        top = jnp.max(scores, 0, keepdims=True)
        weights = jnp.exp2(scores - top).astype(BF)
        if held is not None:
            finish(*held)
        held, scores = (unit, top, weights), later
    finish(*held)


def layer_kernel(
    dims, counts_hbm, route_hbm, tiles_hbm, w_qkv_ref, w_out_ref, out_ref,
    counts_ref, route_ref, tiles_ref, placed, normed_ref, w_qkv, w_out, wq_t, wv_t, wk, wo_t, outgoing, arrived, meta_out, meta_in,
    q_t, keys, v_t, att, near, near_log,
    mid_q, mid_k, mid_v, mid_out, mid_back, wide_qv, wide_k, wide_qv_in, wide_k_in, wide_out, wide_back,
    load_sem, d_send, d_recv, p_send, p_recv, mf_send, mf_recv, wf_send, wf_recv, mb_send, mb_recv,
    wb_send, wb_recv, own_sem,
):
    n_slide, n_seq, most, stride = dims
    owners = n_slide * n_seq
    rows, width = tiles_ref.shape
    half = rows // 2
    run = half // n_seq
    taken = 2 * run
    size = width // HEADS
    duo = 2 * size
    middle_width = width // 2
    factor = math.log2(math.e) / math.sqrt(size)
    slide, seq = lax.axis_index("slide"), lax.axis_index("seq")
    member = seq % GROUP
    group = seq // GROUP
    groups = n_seq // GROUP
    base = seq - member

    def device_at(k):
        return ((slide + k // n_seq) % n_slide, (seq + k % n_seq) % n_seq)

    barrier = pltpu.get_barrier_semaphore()

    def greet(k, carry):
        pl.semaphore_signal(barrier, inc=1, device_id=device_at(k), device_id_type=MESH)
        return carry

    lax.fori_loop(1, owners, greet, 0)
    load_route = pltpu.make_async_copy(route_hbm, route_ref, load_sem.at[2])
    load_tiles = pltpu.make_async_copy(tiles_hbm, tiles_ref, load_sem.at[3])
    load_counts = pltpu.make_async_copy(counts_hbm, counts_ref, load_sem.at[4])
    load_route.start()
    load_tiles.start()
    load_counts.start()
    load_qkv = pltpu.make_async_copy(w_qkv_ref, w_qkv, load_sem.at[0])
    load_out = pltpu.make_async_copy(w_out_ref, w_out, load_sem.at[1])
    load_qkv.start()
    load_out.start()

    if stride > most:
        arrived[:, most:, :] = jnp.zeros((owners, stride - most, width), BF)
    upper = one_hot(iota((rows, rows), 0) <= iota((rows, rows), 1))
    load_route.wait()
    route = route_ref[...]
    owner = route // rows
    offset = ((owner // n_seq - slide + n_slide) % n_slide) * n_seq
    offset = offset + (owner % n_seq - seq + n_seq) % n_seq
    mine = iota((owners, rows), 0) == offset
    counted = dot(one_hot(mine), upper)
    rank = jnp.sum(jnp.where(mine, counted, 0.0), 0, keepdims=True).astype(I32) - 1
    slot = offset * stride + rank
    local = row_of(route % rows, half, n_seq)
    kind = iota((16, rows), 0)
    digits = jnp.where(
        kind == 0, local // 32, jnp.where(kind == 1, local % 32, jnp.where(kind == 2, 1, 0))
    ).astype(F32).astype(BF)

    def dispatch_copy(k):
        return pltpu.make_async_remote_copy(
            src_ref=outgoing.at[k, pl.ds(0, most)], dst_ref=arrived.at[k, pl.ds(0, most)],
            send_sem=d_send.at[k], recv_sem=d_recv.at[k], device_id=device_at(k), device_id_type=MESH,
        )

    per_row = LANES // stride

    def place_copy(k):
        return pltpu.make_async_remote_copy(
            src_ref=meta_out.at[k // per_row], dst_ref=meta_in.at[k],
            send_sem=p_send.at[k], recv_sem=p_recv.at[k], device_id=device_at(k), device_id_type=MESH,
        )

    def start_dispatch(k, carry):
        place_copy(k).start()
        dispatch_copy(k).start()
        return carry

    load_tiles.wait()
    load_counts.wait()
    chunk = 2 * LANES
    blocks = chunk // stride
    steps = owners // blocks

    def make_chunk(c):
        move = one_hot(iota((chunk, rows), 0) + c * chunk == slot)
        sent = dot_nt(digits, move)
        place = sent[0:1] * 32.0 + sent[1:2] + (1.0 - sent[2:3]) * (2.0 * rows)
        for i in range(2):
            meta_out[2 * c + i] = place[:, i * LANES : (i + 1) * LANES]
        moved = dot(move, tiles_ref[...]).astype(BF)
        outgoing[pl.ds(c * blocks, blocks)] = moved.reshape(blocks, stride, width)

    make_chunk(0)
    arrived[0] = outgoing[0]
    meta_in[0] = meta_out[0]
    pl.semaphore_wait(barrier, owners - 1)
    lax.fori_loop(1, blocks, start_dispatch, 0)

    def send_chunk(c, carry):
        make_chunk(c)
        return lax.fori_loop(c * blocks, (c + 1) * blocks, start_dispatch, carry)

    lax.fori_loop(1, steps, send_chunk, 0)
    placed[...] = jnp.zeros((rows, width), BF)
    normed_ref[...] = jnp.zeros((rows, width), BF)

    load_qkv.wait()
    load_out.wait()
    feature = iota((width, width), 0)
    head = (feature % middle_width) // duo + GROUP * (feature // middle_width) + 2 * GROUP * ((feature % duo) // size)
    reorder = one_hot(head * size + feature % size == iota((width, width), 1))
    wq_t[...] = dot_nt(reorder, w_qkv[:, :width]).astype(BF)
    wv_t[...] = dot_nt(reorder, w_qkv[:, 2 * width :]).astype(BF)
    padded = HEADS // 2 * LANES
    column = iota((width, padded), 1)
    pair, lane = column // LANES, column % LANES
    source = (pair + 2 * GROUP * (lane // size)) * size + lane % size
    pick = one_hot((iota((width, padded), 0) == source) & (lane < duo))
    wk[...] = dot(w_qkv[:, width : 2 * width], pick).astype(BF)
    unit_matrix = one_hot(iota((width, width), 0) == iota((width, width), 1))
    wo_t[...] = dot_nt(unit_matrix, dot(reorder, w_out[...]).astype(BF)).astype(BF)

    def wait_dispatch(k, carry):
        place_copy(k).wait_recv()
        dispatch_copy(k).wait_recv()
        return carry

    def places(first, count):
        parts = []
        for i in range(count * 2):
            tile = (2 * first + i) * per_row
            part = meta_in[tile]
            for b in range(1, per_row):
                part = jnp.where(iota((1, LANES), 1) // stride == b, meta_in[tile + b], part)
            parts.append(part)
        return jnp.concatenate(parts, 1).astype(I32)

    def arrivals(first, count):
        return arrived[pl.ds(first * blocks, count * blocks)].reshape(count * chunk, width)

    def spread(place, block):
        return dot(one_hot(iota((rows, place.shape[1]), 0) == place), block).astype(BF)

    def place_rows(first, count):
        placed[...] += spread(position_of(places(first, count), half, n_seq), arrivals(first, count))

    def place_norms(first, count):
        lax.fori_loop(jnp.maximum(1, first * blocks), (first + count) * blocks, wait_dispatch, 0)
        normed_ref[...] += spread(
            places(first, count), layer_norm(arrivals(first, count).astype(F32), 1).astype(BF)
        )

    def place_two(g, carry):
        place_norms(2 * g, 2)
        place_rows(2 * g, 2)
        return carry

    def place_one(g, carry):
        place_norms(g, 1)
        return carry

    lax.fori_loop(0, steps // 2 - 1, place_two, 0)
    lax.fori_loop(steps - 2, steps, place_one, 0)

    limit = counts_ref[slide] - seq * rows

    def pair_at(turn):
        return (group + turn) % 2

    def project(turn):
        j = pair_at(turn)
        part = pl.ds(pl.multiple_of(j * middle_width, middle_width), middle_width)
        columns = pl.ds(pl.multiple_of(j * GROUP * LANES, GROUP * LANES), GROUP * LANES)

        def one_segment(seg, carry):
            normed = normed_ref[pl.ds(seg * half, half), :]
            q = (dot_nt(wq_t[part, :], normed) * factor).astype(BF)
            v = dot_nt(wv_t[part, :], normed).astype(BF)
            for cb in range(GROUP):
                q_t[cb, seg, part, :] = q[:, cb * LANES : (cb + 1) * LANES]
                v_t[cb, seg, part, :] = v[:, cb * LANES : (cb + 1) * LANES]
            at = iota((half, GROUP * LANES), 0) + seg * half
            valid = position_of(at, half, n_seq) < limit
            lane = iota((half, GROUP * LANES), 1) % LANES
            bias = jnp.where((lane == duo) & jnp.logical_not(valid), -1e30, 0.0)
            k = (dot(normed, wk[:, columns]) + bias).astype(BF)
            for o in range(GROUP):
                keys[j, o, seg] = k[:, o * LANES : (o + 1) * LANES]
            return carry

        for seg in range(2):
            one_segment(seg, 0)

    def mid_sources(o, j):
        part = pl.ds(pl.multiple_of(j * middle_width + o * duo, duo), duo)
        return (
            q_t.at[o, :, part, :],
            keys.at[j, o, :, pl.ds(pl.multiple_of(o * LANES, LANES), LANES), :],
            v_t.at[o, :, part, :],
        )

    def mid_copies(k, turn):
        to = (member + k) % GROUP
        return [
            pltpu.make_async_remote_copy(
                src_ref=src, dst_ref=dst.at[turn, k], send_sem=mf_send.at[turn, k, i],
                recv_sem=mf_recv.at[turn, k, i], device_id=(slide, base + to), device_id_type=MESH,
            )
            for i, (src, dst) in enumerate(zip(mid_sources(to, pair_at(turn)), (mid_q, mid_k, mid_v)))
        ]

    def start_mid(turn):
        for k in range(1, GROUP):
            for copy in mid_copies(k, turn):
                copy.start()

    project(0)
    start_mid(0)
    project(1)

    for r in range(n_seq):
        o, j, g = r % GROUP, (r // GROUP) % 2, r // GROUP
        start = j * middle_width + o * duo
        for index, ref in enumerate((q_t, v_t)):
            wide_qv[r, index] = jnp.concatenate(
                [ref[o, seg, start : start + duo, g * run : (g + 1) * run] for seg in range(2)], 1
            )
        for seg in range(2):
            first = o * LANES + g * run
            wide_k[r, seg * run : (seg + 1) * run] = keys[j, o, seg, first : first + run]

    def seq_at(k):
        return (group + k // GROUP) % groups * GROUP + (member + k % GROUP) % GROUP

    def seq_back(k):
        return (group - k // GROUP + groups) % groups * GROUP + (member - k % GROUP + GROUP) % GROUP

    def wide_copies(k):
        to = seq_at(k)
        return [
            pltpu.make_async_remote_copy(
                src_ref=src.at[to], dst_ref=dst.at[k], send_sem=wf_send.at[k, i], recv_sem=wf_recv.at[k, i],
                device_id=(slide, to), device_id_type=MESH,
            )
            for i, (src, dst) in enumerate(((wide_qv, wide_qv_in), (wide_k, wide_k_in)))
        ]

    for k in range(GROUP, n_seq):
        for copy in wide_copies(k):
            copy.start()
    own = [
        pltpu.make_async_copy(src, dst.at[turn, 0], own_sem.at[2 + 3 * turn + i])
        for turn in range(2)
        for i, (src, dst) in enumerate(zip(mid_sources(member, pair_at(turn)), (mid_q, mid_k, mid_v)))
    ]
    for copy in own:
        copy.start()

    def near_owner(o, carry):
        @pl.when(o == 2)
        def _():
            start_mid(1)

        units = []
        for j in range(2):
            for seg in range(2):
                for t in range(2):
                    part = pl.ds(pl.multiple_of(o * duo + (j * middle_width + t * size), TAIL), size)

                    def wide_row(ref, seg=seg, part=part):
                        return jnp.concatenate([ref[cb, seg, part, :] for cb in range(GROUP)], 1)

                    def sink(result, log, j=j, seg=seg, t=t, part=part):
                        for cb in range(GROUP):
                            cut = slice(cb * LANES, (cb + 1) * LANES)
                            att[seg, cb, part, :] = result[:, cut].astype(BF)
                            near[o, j, seg, t, cb] = result[:, cut]
                            near_log[o, j, seg, t, cb] = log[:, cut]

                    units.append((
                        lambda j=j, seg=seg: keys[j, o, seg],
                        lambda wide_row=wide_row: wide_row(q_t),
                        t,
                        lambda wide_row=wide_row: wide_row(v_t),
                        sink,
                    ))
        soft_units(units)
        return carry

    lax.fori_loop(0, GROUP, near_owner, 0)
    place_rows(steps - 2, 2)

    def log_tile(logs, lanes):
        tile = jnp.zeros((TAIL, lanes), F32)
        where = iota((TAIL, lanes), 0)
        for index, piece in enumerate(pieces(logs[0]) + pieces(logs[1])):
            tile = jnp.where(where == index, piece, tile)
        return tile.astype(BF)

    for copy in own:
        copy.wait()

    def mid_return(k, turn):
        return pltpu.make_async_remote_copy(
            src_ref=mid_out.at[turn, k], dst_ref=mid_back.at[member, pair_at(turn)],
            send_sem=mb_send.at[turn, k], recv_sem=mb_recv.at[turn, k],
            device_id=(slide, base + (member - k + GROUP) % GROUP), device_id_type=MESH,
        )

    def wide_return(k):
        return pltpu.make_async_remote_copy(
            src_ref=wide_out.at[k], dst_ref=wide_back.at[seq], send_sem=wb_send.at[k], recv_sem=wb_recv.at[k],
            device_id=(slide, seq_back(k)), device_id_type=MESH,
        )

    def middle(turn):
        units = []
        for slots in ((1, 2), (3, 0)):
            logs = []
            for t in range(2):
                cut = slice(t * size, (t + 1) * size)

                def sink(result, log, t=t, cut=cut, slots=slots, logs=logs):
                    logs.append(log)
                    for index, (k, seg) in enumerate((k, seg) for k in slots for seg in range(2)):
                        lanes = slice(index * LANES, (index + 1) * LANES)
                        mid_out[turn, k, seg, cut] = result[:, lanes].astype(BF)
                        if t == 1:
                            mid_out[turn, k, seg, duo:] = log_tile([one[:, lanes] for one in logs], LANES)
                    if t == 1:
                        for k in slots:
                            if k:
                                mid_return(k, turn).start()

                units.append((
                    lambda: mid_k[turn].reshape(rows, LANES),
                    lambda slots=slots, cut=cut: jnp.concatenate(
                        [mid_q[turn, k, seg, cut] for k in slots for seg in range(2)], 1
                    ),
                    t,
                    lambda cut=cut: jnp.concatenate(
                        [mid_v[turn, k, seg, cut] for k in range(GROUP) for seg in range(2)], 1
                    ),
                    sink,
                ))
        return units

    def widest():
        order = [k % n_seq for k in range(1, n_seq + 1)]
        count = n_seq // 2
        units = []
        for part in range(2):
            slots = order[part * count : (part + 1) * count]
            logs = []
            for t in range(2):
                cut = slice(t * size, (t + 1) * size)

                def sink(result, log, t=t, slots=slots, cut=cut, logs=logs):
                    logs.append(log)
                    for index, k in enumerate(slots):
                        lanes = slice(index * taken, (index + 1) * taken)
                        wide_out[k, cut] = result[:, lanes].astype(BF)
                        if t == 1:
                            wide_out[k, duo:] = log_tile([one[:, lanes] for one in logs], taken)
                            if k:
                                wide_return(k).start()

                units.append((
                    lambda: wide_k_in[...].reshape(n_seq * taken, LANES),
                    lambda slots=slots, cut=cut: jnp.concatenate([wide_qv_in[k, 0, cut] for k in slots], 1),
                    t,
                    lambda cut=cut: jnp.concatenate([wide_qv_in[k, 1, cut] for k in range(n_seq)], 1),
                    sink,
                ))
        return units

    for k in range(1, GROUP):
        for copy in mid_copies(k, 0):
            copy.wait_recv()
    for k in range(GROUP):
        for index, ref in enumerate((mid_q, mid_v)):
            first, second = ref[0, k, 0], ref[0, k, 1]
            own_part = None
            for g in range(groups):
                lanes = slice(g * run, (g + 1) * run)
                part = jnp.concatenate([first[:, lanes], second[:, lanes]], 1)
                own_part = part if g == 0 else jnp.where(group == g, part, own_part)
            wide_qv_in[k, index] = own_part
        for seg in range(2):
            wide_k_in[k, seg * run : (seg + 1) * run] = mid_k[0, k, seg, pl.ds(pl.multiple_of(group * run, run), run)]
    soft_units(middle(0))
    for k in range(GROUP, n_seq):
        for copy in wide_copies(k):
            copy.wait_recv()
    soft_units(widest())
    own_wide = pltpu.make_async_copy(wide_out.at[0], wide_back.at[seq], own_sem.at[0])
    own_wide.start()
    for k in range(1, GROUP):
        for copy in mid_copies(k, 1):
            copy.wait_recv()
    soft_units(middle(1))
    own_mid = [
        pltpu.make_async_copy(mid_out.at[turn, 0], mid_back.at[member, pair_at(turn)], own_sem.at[1 + turn])
        for turn in range(2)
    ]
    for copy in own_mid:
        copy.start()

    own_wide.wait()
    for copy in own_mid:
        copy.wait()
    for k in range(1, n_seq):
        wide_return(k).wait_recv()
    for k in range(1, GROUP):
        for turn in range(2):
            mid_return(k, turn).wait_recv()

    def log_of(tile, t):
        return tile[3 * t : 3 * t + 1] + tile[3 * t + 1 : 3 * t + 2] + tile[3 * t + 2 : 3 * t + 3]

    def embed(value, g, fill):
        before = [jnp.full((value.shape[0], g * run), fill, F32)] if g else []
        after = LANES - (g + 1) * run
        behind = [jnp.full((value.shape[0], after), fill, F32)] if after else []
        return jnp.concatenate(before + [value] + behind, 1)

    def merge_owner(o, carry):
        for j in range(2):
            for t in range(2):
                first = (GROUP * j + 2 * GROUP * t) % n_seq
                wide = wide_back[first + o].astype(F32)
                cut = slice(t * size, (t + 1) * size)
                rows_of = pl.ds(o * duo + (j * middle_width + t * size), size)
                for seg in range(2):
                    lanes = slice(seg * run, (seg + 1) * run)
                    wide_o = embed(wide[cut, lanes], first // GROUP, 0.0)
                    log_w = embed(log_of(wide[duo:, lanes], t), first // GROUP, -3e30)
                    mid = mid_back[o, j, seg].astype(F32)
                    log_m = log_of(mid[duo:], t)
                    log_n = near_log[o, j, seg, t, o]
                    top = jnp.maximum(jnp.maximum(log_n, log_m), log_w)
                    share_n, share_m, share_w = jnp.exp2(log_n - top), jnp.exp2(log_m - top), jnp.exp2(log_w - top)
                    scale = 1.0 / (share_n + share_m + share_w)
                    merged = (
                        near[o, j, seg, t, o] * (share_n * scale)
                        + mid[cut] * (share_m * scale)
                        + wide_o * (share_w * scale)
                    )
                    att[seg, o, rows_of, :] = merged.astype(BF)
        return carry

    for o in range(GROUP):
        merge_owner(o, 0)

    unsort = one_hot(row_of(iota((half, half), 0), half, n_seq) == iota((half, half), 1))

    def store(seg):
        part = pl.ds(seg * half, half)
        return pltpu.make_async_copy(tiles_ref.at[part], out_ref.at[part], load_sem.at[seg])

    def finish_segment(seg, carry):
        part = pl.ds(seg * half, half)
        attended = jnp.concatenate([att[seg, cb] for cb in range(GROUP)], 1)
        normed = layer_norm(dot(wo_t[...], attended), 0).astype(BF)
        value = dot_nt(unsort, normed) + placed[part, :].astype(F32)
        position = iota((half, width), 0) + seg * half
        tiles_ref[part, :] = jnp.where(position < limit, value, 0.0).astype(BF)
        store(seg).start()
        return carry

    for seg in range(2):
        finish_segment(seg, 0)

    def drain(k, carry):
        place_copy(k).wait_send()
        dispatch_copy(k).wait_send()
        return carry

    lax.fori_loop(1, owners, drain, 0)
    for k in range(1, n_seq):
        if k >= GROUP:
            for copy in wide_copies(k):
                copy.wait_send()
        wide_return(k).wait_send()
    for k in range(1, GROUP):
        for turn in range(2):
            for copy in mid_copies(k, turn):
                copy.wait_send()
            mid_return(k, turn).wait_send()
    for seg in range(2):
        store(seg).wait()


def body(tiles, route, counts, w_qkv, w_out):
    rows, width = tiles.shape
    n_slide = lax.axis_size("slide")
    n_seq = lax.axis_size("seq")
    owners = n_slide * n_seq
    most = -(-(3 * rows // (2 * owners)) // 16) * 16
    stride = 1 << (most - 1).bit_length()
    half = rows // 2
    taken = rows // n_seq
    size = width // HEADS
    duo = 2 * size
    back = duo + TAIL
    dma = pltpu.SemaphoreType.DMA

    def buffer(*shape, dtype=BF):
        return pltpu.VMEM(shape, dtype)

    return pl.pallas_call(
        functools.partial(layer_kernel, (n_slide, n_seq, most, stride)),
        out_shape=jax.ShapeDtypeStruct((rows, width), BF),
        in_specs=[
            pl.BlockSpec(memory_space=pl.ANY),
        ] * 5,
        out_specs=pl.BlockSpec(memory_space=pl.ANY),
        scratch_shapes=[
            pltpu.SMEM((n_slide,), I32),
            buffer(1, rows, dtype=I32),
            buffer(rows, width),
            buffer(rows, width),
            buffer(rows, width),
            buffer(width, 3 * width),
            buffer(width, width),
            buffer(width, width),
            buffer(width, width),
            buffer(width, HEADS // 2 * LANES),
            buffer(width, width),
            buffer(owners, stride, width),
            buffer(owners, stride, width),
            buffer(owners * stride // LANES, 1, LANES, dtype=F32),
            buffer(owners, 1, LANES, dtype=F32),
            buffer(GROUP, 2, width, LANES),
            buffer(2, GROUP, 2, half, LANES),
            buffer(GROUP, 2, width, LANES),
            buffer(2, GROUP, width, LANES),
            buffer(GROUP, 2, 2, 2, GROUP, size, LANES, dtype=F32),
            buffer(GROUP, 2, 2, 2, GROUP, 1, LANES, dtype=F32),
            buffer(2, GROUP, 2, duo, LANES),
            buffer(2, GROUP, 2, LANES, LANES),
            buffer(2, GROUP, 2, duo, LANES),
            buffer(2, GROUP, 2, back, LANES),
            buffer(GROUP, 2, 2, back, LANES),
            buffer(n_seq, 2, duo, taken),
            buffer(n_seq, taken, LANES),
            buffer(n_seq, 2, duo, taken),
            buffer(n_seq, taken, LANES),
            buffer(n_seq, back, taken),
            buffer(n_seq, back, taken),
            dma((5,)),
            dma((owners,)), dma((owners,)), dma((owners,)), dma((owners,)),
            dma((2, GROUP, 3)), dma((2, GROUP, 3)), dma((n_seq, 2)), dma((n_seq, 2)),
            dma((2, GROUP)), dma((2, GROUP)), dma((n_seq,)), dma((n_seq,)),
            dma((8,)),
        ],
        compiler_params=pltpu.CompilerParams(
            collective_id=0, has_side_effects=True, vmem_limit_bytes=58 << 20
        ),
        name="layer",
    )(counts, route.reshape(1, rows), tiles, w_qkv, w_out)


def solution(mesh):
    return jax.shard_map(
        body,
        mesh=mesh,
        in_specs=(P(("slide", "seq"), None), P(("slide", "seq")), P(), P(), P()),
        out_specs=P(("slide", "seq"), None),
        check_vma=False,
    )
```

```python
import functools
import math

import jax
import jax.numpy as jnp
from jax import lax
from jax.experimental import pallas as pl
from jax.experimental.pallas import tpu as pltpu
from jax.sharding import PartitionSpec as P

HEADS = 16
GROUP = 4
LANES = 128
TAIL = 16
BF = jnp.bfloat16
F32 = jnp.float32
I32 = jnp.int32
MESH = pl.DeviceIdType.MESH


def iota(shape, dim):
    return lax.broadcasted_iota(I32, shape, dim)


def dot(a, b):
    return jnp.dot(a, b, preferred_element_type=F32)


def dot_nt(a, b):
    return lax.dot_general(a, b, (((1,), (1,)), ((), ())), preferred_element_type=F32)


def one_hot(condition):
    return jnp.where(condition, 1.0, 0.0).astype(BF)


def position_of(row, half, n_seq):
    run = half // n_seq
    block = (row % half) // run
    groups = n_seq // GROUP
    residue = (block % groups) * GROUP + block // groups
    return (row // half) * half + (row % run) * n_seq + residue


def row_of(position, half, n_seq):
    run = half // n_seq
    within = position % half
    residue = within % n_seq
    block = (residue % GROUP) * (n_seq // GROUP) + residue // GROUP
    return (position // half) * half + block * run + within // n_seq


def layer_norm(values, axis):
    mean = jnp.mean(values, axis, keepdims=True)
    centred = values - mean
    var = jnp.mean(centred * centred, axis, keepdims=True)
    return centred * lax.rsqrt(var + 1e-05)


def pieces(value):
    first = value.astype(BF).astype(F32)
    second = (value - first).astype(BF).astype(F32)
    return first, second, value - first - second


def soft_units(units):
    def score(unit):
        keys, query, head, _, _ = unit
        q = query()
        width = q.shape[1]
        zero = jnp.zeros(q.shape, BF)
        flag = one_hot(iota((32, width), 0) == 0)
        return dot(keys(), jnp.concatenate(([q, zero] if head == 0 else [zero, q]) + [flag], 0))

    def finish(unit, top, weights):
        values, sink = unit[3], unit[4]
        v = values()
        both = jnp.concatenate([v, jnp.ones((TAIL, v.shape[1]), BF)], 0)
        result = dot(both, weights)
        size = v.shape[0]
        total = result[size : size + 1]
        sink(result[:size] * (1.0 / total), top + jnp.log2(total))

    scores, held = score(units[0]), None
    for index, unit in enumerate(units):
        later = score(units[index + 1]) if index + 1 < len(units) else None
        top = jnp.max(scores, 0, keepdims=True)
        weights = jnp.exp2(scores - top).astype(BF)
        if held is not None:
            finish(*held)
        held, scores = (unit, top, weights), later
    finish(*held)


def layer_kernel(
    dims, counts_hbm, route_hbm, tiles_hbm, w_qkv_ref, w_out_ref, out_ref,
    counts_ref, route_ref, tiles_ref, placed, normed_ref, w_qkv, w_out, wq_t, wv_t, wk, wo_t, outgoing, arrived, meta_out, meta_in,
    q_t, keys, v_t, att, near, near_log,
    mid_q, mid_k, mid_v, mid_out, mid_back, wide_qv, wide_k, wide_qv_in, wide_k_in, wide_out, wide_back,
    load_sem, d_send, d_recv, p_send, p_recv, mf_send, mf_recv, wf_send, wf_recv, mb_send, mb_recv,
    wb_send, wb_recv, own_sem,
):
    n_slide, n_seq, most, stride = dims
    owners = n_slide * n_seq
    rows, width = tiles_ref.shape
    half = rows // 2
    run = half // n_seq
    taken = 2 * run
    size = width // HEADS
    duo = 2 * size
    middle_width = width // 2
    factor = math.log2(math.e) / math.sqrt(size)
    slide, seq = lax.axis_index("slide"), lax.axis_index("seq")
    member = seq % GROUP
    group = seq // GROUP
    groups = n_seq // GROUP
    base = seq - member

    def device_at(k):
        return ((slide + k // n_seq) % n_slide, (seq + k % n_seq) % n_seq)

    barrier = pltpu.get_barrier_semaphore()

    def greet(k, carry):
        pl.semaphore_signal(barrier, inc=1, device_id=device_at(k), device_id_type=MESH)
        return carry

    lax.fori_loop(1, owners, greet, 0)
    load_route = pltpu.make_async_copy(route_hbm, route_ref, load_sem.at[2])
    load_tiles = pltpu.make_async_copy(tiles_hbm, tiles_ref, load_sem.at[3])
    load_counts = pltpu.make_async_copy(counts_hbm, counts_ref, load_sem.at[4])
    load_route.start()
    load_tiles.start()
    load_counts.start()
    load_qkv = pltpu.make_async_copy(w_qkv_ref, w_qkv, load_sem.at[0])
    load_out = pltpu.make_async_copy(w_out_ref, w_out, load_sem.at[1])
    load_qkv.start()
    load_out.start()

    if stride > most:
        arrived[:, most:, :] = jnp.zeros((owners, stride - most, width), BF)
    upper = one_hot(iota((rows, rows), 0) <= iota((rows, rows), 1))
    load_route.wait()
    route = route_ref[...]
    owner = route // rows
    offset = ((owner // n_seq - slide + n_slide) % n_slide) * n_seq
    offset = offset + (owner % n_seq - seq + n_seq) % n_seq
    mine = iota((owners, rows), 0) == offset
    counted = dot(one_hot(mine), upper)
    rank = jnp.sum(jnp.where(mine, counted, 0.0), 0, keepdims=True).astype(I32) - 1
    slot = offset * stride + rank
    local = row_of(route % rows, half, n_seq)
    kind = iota((16, rows), 0)
    digits = jnp.where(
        kind == 0, local // 32, jnp.where(kind == 1, local % 32, jnp.where(kind == 2, 1, 0))
    ).astype(F32).astype(BF)

    def dispatch_copy(k):
        return pltpu.make_async_remote_copy(
            src_ref=outgoing.at[k, pl.ds(0, most)], dst_ref=arrived.at[k, pl.ds(0, most)],
            send_sem=d_send.at[k], recv_sem=d_recv.at[k], device_id=device_at(k), device_id_type=MESH,
        )

    per_row = LANES // stride

    def place_copy(k):
        return pltpu.make_async_remote_copy(
            src_ref=meta_out.at[k // per_row], dst_ref=meta_in.at[k],
            send_sem=p_send.at[k], recv_sem=p_recv.at[k], device_id=device_at(k), device_id_type=MESH,
        )

    def start_dispatch(k, carry):
        place_copy(k).start()
        dispatch_copy(k).start()
        return carry

    load_tiles.wait()
    load_counts.wait()
    chunk = 2 * LANES
    blocks = chunk // stride
    steps = owners // blocks

    def make_chunk(c):
        move = one_hot(iota((chunk, rows), 0) + c * chunk == slot)
        sent = dot_nt(digits, move)
        place = sent[0:1] * 32.0 + sent[1:2] + (1.0 - sent[2:3]) * (2.0 * rows)
        for i in range(2):
            meta_out[2 * c + i] = place[:, i * LANES : (i + 1) * LANES]
        moved = dot(move, tiles_ref[...]).astype(BF)
        outgoing[pl.ds(c * blocks, blocks)] = moved.reshape(blocks, stride, width)

    make_chunk(0)
    arrived[0] = outgoing[0]
    meta_in[0] = meta_out[0]
    pl.semaphore_wait(barrier, owners - 1)
    lax.fori_loop(1, blocks, start_dispatch, 0)

    def send_chunk(c, carry):
        make_chunk(c)
        return lax.fori_loop(c * blocks, (c + 1) * blocks, start_dispatch, carry)

    lax.fori_loop(1, steps, send_chunk, 0)
    placed[...] = jnp.zeros((rows, width), BF)
    normed_ref[...] = jnp.zeros((rows, width), BF)

    load_qkv.wait()
    load_out.wait()
    feature = iota((width, width), 0)
    head = (feature % middle_width) // duo + GROUP * (feature // middle_width) + 2 * GROUP * ((feature % duo) // size)
    reorder = one_hot(head * size + feature % size == iota((width, width), 1))
    wq_t[...] = dot_nt(reorder, w_qkv[:, :width]).astype(BF)
    wv_t[...] = dot_nt(reorder, w_qkv[:, 2 * width :]).astype(BF)
    padded = HEADS // 2 * LANES
    column = iota((width, padded), 1)
    pair, lane = column // LANES, column % LANES
    source = (pair + 2 * GROUP * (lane // size)) * size + lane % size
    pick = one_hot((iota((width, padded), 0) == source) & (lane < duo))
    wk[...] = dot(w_qkv[:, width : 2 * width], pick).astype(BF)
    unit_matrix = one_hot(iota((width, width), 0) == iota((width, width), 1))
    wo_t[...] = dot_nt(unit_matrix, dot(reorder, w_out[...]).astype(BF)).astype(BF)

    def wait_dispatch(k, carry):
        place_copy(k).wait_recv()
        dispatch_copy(k).wait_recv()
        return carry

    def places(first, count):
        parts = []
        for i in range(count * 2):
            tile = (2 * first + i) * per_row
            part = meta_in[tile]
            for b in range(1, per_row):
                part = jnp.where(iota((1, LANES), 1) // stride == b, meta_in[tile + b], part)
            parts.append(part)
        return jnp.concatenate(parts, 1).astype(I32)

    def arrivals(first, count):
        return arrived[pl.ds(first * blocks, count * blocks)].reshape(count * chunk, width)

    def spread(place, block):
        return dot(one_hot(iota((rows, place.shape[1]), 0) == place), block).astype(BF)

    def place_rows(first, count):
        placed[...] += spread(position_of(places(first, count), half, n_seq), arrivals(first, count))

    def place_norms(first, count):
        lax.fori_loop(jnp.maximum(1, first * blocks), (first + count) * blocks, wait_dispatch, 0)
        normed_ref[...] += spread(
            places(first, count), layer_norm(arrivals(first, count).astype(F32), 1).astype(BF)
        )

    def place_two(g, carry):
        place_norms(2 * g, 2)
        place_rows(2 * g, 2)
        return carry

    def place_one(g, carry):
        place_norms(g, 1)
        return carry

    lax.fori_loop(0, steps // 2 - 1, place_two, 0)
    lax.fori_loop(steps - 2, steps, place_one, 0)

    limit = counts_ref[slide] - seq * rows

    def pair_at(turn):
        return (group + turn) % 2

    def project(turn):
        j = pair_at(turn)
        part = pl.ds(pl.multiple_of(j * middle_width, middle_width), middle_width)
        columns = pl.ds(pl.multiple_of(j * GROUP * LANES, GROUP * LANES), GROUP * LANES)

        def one_segment(seg, carry):
            normed = normed_ref[pl.ds(seg * half, half), :]
            q = (dot_nt(wq_t[part, :], normed) * factor).astype(BF)
            v = dot_nt(wv_t[part, :], normed).astype(BF)
            for cb in range(GROUP):
                q_t[cb, seg, part, :] = q[:, cb * LANES : (cb + 1) * LANES]
                v_t[cb, seg, part, :] = v[:, cb * LANES : (cb + 1) * LANES]
            at = iota((half, GROUP * LANES), 0) + seg * half
            valid = position_of(at, half, n_seq) < limit
            lane = iota((half, GROUP * LANES), 1) % LANES
            bias = jnp.where((lane == duo) & jnp.logical_not(valid), -1e30, 0.0)
            k = (dot(normed, wk[:, columns]) + bias).astype(BF)
            for o in range(GROUP):
                keys[j, o, seg] = k[:, o * LANES : (o + 1) * LANES]
            return carry

        for seg in range(2):
            one_segment(seg, 0)
            if turn == 0:
                start_mid(0, seg)

    def mid_sources(o, j, seg):
        part = pl.ds(pl.multiple_of(j * middle_width + o * duo, duo), duo)
        return (
            q_t.at[o, seg, part, :],
            keys.at[j, o, seg, pl.ds(pl.multiple_of(o * LANES, LANES), LANES), :],
            v_t.at[o, seg, part, :],
        )

    def mid_copies(k, turn, seg):
        to = (member + k) % GROUP
        return [
            pltpu.make_async_remote_copy(
                src_ref=src, dst_ref=dst.at[turn, k, seg], send_sem=mf_send.at[turn, k, seg, i],
                recv_sem=mf_recv.at[turn, k, seg, i], device_id=(slide, base + to), device_id_type=MESH,
            )
            for i, (src, dst) in enumerate(zip(mid_sources(to, pair_at(turn), seg), (mid_q, mid_k, mid_v)))
        ]

    def start_mid(turn, seg):
        for k in range(1, GROUP):
            for copy in mid_copies(k, turn, seg):
                copy.start()

    project(0)
    project(1)

    for r in range(n_seq):
        o, j, g = r % GROUP, (r // GROUP) % 2, r // GROUP
        start = j * middle_width + o * duo
        for index, ref in enumerate((q_t, v_t)):
            wide_qv[r, index] = jnp.concatenate(
                [ref[o, seg, start : start + duo, g * run : (g + 1) * run] for seg in range(2)], 1
            )
        for seg in range(2):
            first = o * LANES + g * run
            wide_k[r, seg * run : (seg + 1) * run] = keys[j, o, seg, first : first + run]

    def seq_at(k):
        return (group + k // GROUP) % groups * GROUP + (member + k % GROUP) % GROUP

    def seq_back(k):
        return (group - k // GROUP + groups) % groups * GROUP + (member - k % GROUP + GROUP) % GROUP

    def wide_copies(k):
        to = seq_at(k)
        return [
            pltpu.make_async_remote_copy(
                src_ref=src.at[to], dst_ref=dst.at[k], send_sem=wf_send.at[k, i], recv_sem=wf_recv.at[k, i],
                device_id=(slide, to), device_id_type=MESH,
            )
            for i, (src, dst) in enumerate(((wide_qv, wide_qv_in), (wide_k, wide_k_in)))
        ]

    for k in range(GROUP, n_seq):
        for copy in wide_copies(k):
            copy.start()
    own = [
        pltpu.make_async_copy(src, dst.at[turn, 0, seg], own_sem.at[5 + 6 * turn + 3 * seg + i])
        for turn in range(2)
        for seg in range(2)
        for i, (src, dst) in enumerate(zip(mid_sources(member, pair_at(turn), seg), (mid_q, mid_k, mid_v)))
    ]
    for copy in own:
        copy.start()

    def near_owner(o, carry):
        @pl.when(o == 2)
        def _():
            for seg in range(2):
                start_mid(1, seg)

        units = []
        for j in range(2):
            for seg in range(2):
                for t in range(2):
                    part = pl.ds(pl.multiple_of(o * duo + (j * middle_width + t * size), TAIL), size)

                    def wide_row(ref, seg=seg, part=part):
                        return jnp.concatenate([ref[cb, seg, part, :] for cb in range(GROUP)], 1)

                    def sink(result, log, j=j, seg=seg, t=t, part=part):
                        for cb in range(GROUP):
                            cut = slice(cb * LANES, (cb + 1) * LANES)
                            att[seg, cb, part, :] = result[:, cut].astype(BF)
                            near[o, j, seg, t, cb] = result[:, cut]
                            near_log[o, j, seg, t, cb] = log[:, cut]

                    units.append((
                        lambda j=j, seg=seg: keys[j, o, seg],
                        lambda wide_row=wide_row: wide_row(q_t),
                        t,
                        lambda wide_row=wide_row: wide_row(v_t),
                        sink,
                    ))
        soft_units(units)
        return carry

    lax.fori_loop(0, GROUP, near_owner, 0)

    def log_tile(logs, lanes):
        tile = jnp.zeros((TAIL, lanes), F32)
        where = iota((TAIL, lanes), 0)
        for index, piece in enumerate(pieces(logs[0]) + pieces(logs[1])):
            tile = jnp.where(where == index, piece, tile)
        return tile.astype(BF)

    for copy in own:
        copy.wait()

    def mid_return(k, turn, seg):
        return pltpu.make_async_remote_copy(
            src_ref=mid_out.at[turn, k, seg], dst_ref=mid_back.at[member, pair_at(turn), seg],
            send_sem=mb_send.at[turn, k, seg], recv_sem=mb_recv.at[turn, k, seg],
            device_id=(slide, base + (member - k + GROUP) % GROUP), device_id_type=MESH,
        )

    def wide_return(k):
        return pltpu.make_async_remote_copy(
            src_ref=wide_out.at[k], dst_ref=wide_back.at[seq], send_sem=wb_send.at[k], recv_sem=wb_recv.at[k],
            device_id=(slide, seq_back(k)), device_id_type=MESH,
        )

    def middle(turn):
        slots = (1, 2, 3, 0)
        units = []
        for seg in range(2):
            logs = []
            for t in range(2):
                cut = slice(t * size, (t + 1) * size)

                def sink(result, log, t=t, cut=cut, seg=seg, logs=logs):
                    logs.append(log)
                    for index, k in enumerate(slots):
                        lanes = slice(index * LANES, (index + 1) * LANES)
                        mid_out[turn, k, seg, cut] = result[:, lanes].astype(BF)
                        if t == 1:
                            mid_out[turn, k, seg, duo:] = log_tile([one[:, lanes] for one in logs], LANES)
                            if k:
                                mid_return(k, turn, seg).start()

                units.append((
                    lambda: mid_k[turn].reshape(rows, LANES),
                    lambda seg=seg, cut=cut: jnp.concatenate([mid_q[turn, k, seg, cut] for k in slots], 1),
                    t,
                    lambda cut=cut: jnp.concatenate(
                        [mid_v[turn, k, seg, cut] for k in range(GROUP) for seg in range(2)], 1
                    ),
                    sink,
                ))
        return units

    def widest():
        order = [k % n_seq for k in range(1, n_seq + 1)]
        count = n_seq // 2
        units = []
        for part in range(2):
            slots = order[part * count : (part + 1) * count]
            logs = []
            for t in range(2):
                cut = slice(t * size, (t + 1) * size)

                def sink(result, log, t=t, slots=slots, cut=cut, logs=logs):
                    logs.append(log)
                    for index, k in enumerate(slots):
                        lanes = slice(index * taken, (index + 1) * taken)
                        wide_out[k, cut] = result[:, lanes].astype(BF)
                        if t == 1:
                            wide_out[k, duo:] = log_tile([one[:, lanes] for one in logs], taken)
                            if k:
                                wide_return(k).start()

                units.append((
                    lambda: wide_k_in[...].reshape(n_seq * taken, LANES),
                    lambda slots=slots, cut=cut: jnp.concatenate([wide_qv_in[k, 0, cut] for k in slots], 1),
                    t,
                    lambda cut=cut: jnp.concatenate([wide_qv_in[k, 1, cut] for k in range(n_seq)], 1),
                    sink,
                ))
        return units

    for k in range(1, GROUP):
        for seg in range(2):
            for copy in mid_copies(k, 0, seg):
                copy.wait_recv()
    for k in range(GROUP):
        for index, ref in enumerate((mid_q, mid_v)):
            first, second = ref[0, k, 0], ref[0, k, 1]
            own_part = None
            for g in range(groups):
                lanes = slice(g * run, (g + 1) * run)
                part = jnp.concatenate([first[:, lanes], second[:, lanes]], 1)
                own_part = part if g == 0 else jnp.where(group == g, part, own_part)
            wide_qv_in[k, index] = own_part
        for seg in range(2):
            wide_k_in[k, seg * run : (seg + 1) * run] = mid_k[0, k, seg, pl.ds(pl.multiple_of(group * run, run), run)]
    soft_units(middle(0))
    for k in range(GROUP, n_seq):
        for copy in wide_copies(k):
            copy.wait_recv()
    soft_units(widest())
    own_wide = pltpu.make_async_copy(wide_out.at[0], wide_back.at[seq], own_sem.at[0])
    own_wide.start()
    place_rows(steps - 2, 2)
    for k in range(1, GROUP):
        for seg in range(2):
            for copy in mid_copies(k, 1, seg):
                copy.wait_recv()
    soft_units(middle(1))
    own_mid = [
        pltpu.make_async_copy(
            mid_out.at[turn, 0, seg], mid_back.at[member, pair_at(turn), seg], own_sem.at[1 + 2 * turn + seg]
        )
        for turn in range(2)
        for seg in range(2)
    ]
    for copy in own_mid:
        copy.start()

    own_wide.wait()
    for copy in own_mid:
        copy.wait()
    for k in range(1, n_seq):
        wide_return(k).wait_recv()

    def log_of(tile, t):
        return tile[3 * t : 3 * t + 1] + tile[3 * t + 1 : 3 * t + 2] + tile[3 * t + 2 : 3 * t + 3]

    def embed(value, g, fill):
        before = [jnp.full((value.shape[0], g * run), fill, F32)] if g else []
        after = LANES - (g + 1) * run
        behind = [jnp.full((value.shape[0], after), fill, F32)] if after else []
        return jnp.concatenate(before + [value] + behind, 1)

    def merge_owner(o, seg):
        for j in range(2):
            for t in range(2):
                first = (GROUP * j + 2 * GROUP * t) % n_seq
                wide = wide_back[first + o].astype(F32)
                cut = slice(t * size, (t + 1) * size)
                rows_of = pl.ds(o * duo + (j * middle_width + t * size), size)
                lanes = slice(seg * run, (seg + 1) * run)
                wide_o = embed(wide[cut, lanes], first // GROUP, 0.0)
                log_w = embed(log_of(wide[duo:, lanes], t), first // GROUP, -3e30)
                mid = mid_back[o, j, seg].astype(F32)
                log_m = log_of(mid[duo:], t)
                log_n = near_log[o, j, seg, t, o]
                top = jnp.maximum(jnp.maximum(log_n, log_m), log_w)
                share_n, share_m, share_w = jnp.exp2(log_n - top), jnp.exp2(log_m - top), jnp.exp2(log_w - top)
                scale = 1.0 / (share_n + share_m + share_w)
                merged = (
                    near[o, j, seg, t, o] * (share_n * scale)
                    + mid[cut] * (share_m * scale)
                    + wide_o * (share_w * scale)
                )
                att[seg, o, rows_of, :] = merged.astype(BF)

    unsort = one_hot(row_of(iota((half, half), 0), half, n_seq) == iota((half, half), 1))

    def store(seg):
        part = pl.ds(seg * half, half)
        return pltpu.make_async_copy(tiles_ref.at[part], out_ref.at[part], load_sem.at[seg])

    def finish_segment(seg, carry):
        part = pl.ds(seg * half, half)
        attended = jnp.concatenate([att[seg, cb] for cb in range(GROUP)], 1)
        normed = layer_norm(dot(wo_t[...], attended), 0).astype(BF)
        value = dot_nt(unsort, normed) + placed[part, :].astype(F32)
        position = iota((half, width), 0) + seg * half
        tiles_ref[part, :] = jnp.where(position < limit, value, 0.0).astype(BF)
        store(seg).start()
        return carry

    for seg in range(2):
        for k in range(1, GROUP):
            for turn in range(2):
                mid_return(k, turn, seg).wait_recv()
        for o in range(GROUP):
            merge_owner(o, seg)
        finish_segment(seg, 0)

    def drain(k, carry):
        place_copy(k).wait_send()
        dispatch_copy(k).wait_send()
        return carry

    lax.fori_loop(1, owners, drain, 0)
    for k in range(1, n_seq):
        if k >= GROUP:
            for copy in wide_copies(k):
                copy.wait_send()
        wide_return(k).wait_send()
    for k in range(1, GROUP):
        for turn in range(2):
            for seg in range(2):
                for copy in mid_copies(k, turn, seg):
                    copy.wait_send()
                mid_return(k, turn, seg).wait_send()
    for seg in range(2):
        store(seg).wait()


def body(tiles, route, counts, w_qkv, w_out):
    rows, width = tiles.shape
    n_slide = lax.axis_size("slide")
    n_seq = lax.axis_size("seq")
    owners = n_slide * n_seq
    most = -(-(3 * rows // (2 * owners)) // 16) * 16
    stride = 1 << (most - 1).bit_length()
    half = rows // 2
    taken = rows // n_seq
    size = width // HEADS
    duo = 2 * size
    back = duo + TAIL
    dma = pltpu.SemaphoreType.DMA

    def buffer(*shape, dtype=BF):
        return pltpu.VMEM(shape, dtype)

    return pl.pallas_call(
        functools.partial(layer_kernel, (n_slide, n_seq, most, stride)),
        out_shape=jax.ShapeDtypeStruct((rows, width), BF),
        in_specs=[
            pl.BlockSpec(memory_space=pl.ANY),
        ] * 5,
        out_specs=pl.BlockSpec(memory_space=pl.ANY),
        scratch_shapes=[
            pltpu.SMEM((n_slide,), I32),
            buffer(1, rows, dtype=I32),
            buffer(rows, width),
            buffer(rows, width),
            buffer(rows, width),
            buffer(width, 3 * width),
            buffer(width, width),
            buffer(width, width),
            buffer(width, width),
            buffer(width, HEADS // 2 * LANES),
            buffer(width, width),
            buffer(owners, stride, width),
            buffer(owners, stride, width),
            buffer(owners * stride // LANES, 1, LANES, dtype=F32),
            buffer(owners, 1, LANES, dtype=F32),
            buffer(GROUP, 2, width, LANES),
            buffer(2, GROUP, 2, half, LANES),
            buffer(GROUP, 2, width, LANES),
            buffer(2, GROUP, width, LANES),
            buffer(GROUP, 2, 2, 2, GROUP, size, LANES, dtype=F32),
            buffer(GROUP, 2, 2, 2, GROUP, 1, LANES, dtype=F32),
            buffer(2, GROUP, 2, duo, LANES),
            buffer(2, GROUP, 2, LANES, LANES),
            buffer(2, GROUP, 2, duo, LANES),
            buffer(2, GROUP, 2, back, LANES),
            buffer(GROUP, 2, 2, back, LANES),
            buffer(n_seq, 2, duo, taken),
            buffer(n_seq, taken, LANES),
            buffer(n_seq, 2, duo, taken),
            buffer(n_seq, taken, LANES),
            buffer(n_seq, back, taken),
            buffer(n_seq, back, taken),
            dma((5,)),
            dma((owners,)), dma((owners,)), dma((owners,)), dma((owners,)),
            dma((2, GROUP, 2, 3)), dma((2, GROUP, 2, 3)), dma((n_seq, 2)), dma((n_seq, 2)),
            dma((2, GROUP, 2)), dma((2, GROUP, 2)), dma((n_seq,)), dma((n_seq,)),
            dma((17,)),
        ],
        compiler_params=pltpu.CompilerParams(
            collective_id=0, has_side_effects=True, vmem_limit_bytes=58 << 20
        ),
        name="layer",
    )(counts, route.reshape(1, rows), tiles, w_qkv, w_out)


def solution(mesh):
    return jax.shard_map(
        body,
        mesh=mesh,
        in_specs=(P(("slide", "seq"), None), P(("slide", "seq")), P(), P(), P()),
        out_specs=P(("slide", "seq"), None),
        check_vma=False,
    )
```

```python
import functools
import math

import jax
import jax.numpy as jnp
from jax import lax
from jax.experimental import pallas as pl
from jax.experimental.pallas import tpu as pltpu
from jax.sharding import PartitionSpec as P

HEADS = 16
GROUP = 4
LANES = 128
TAIL = 16
BF = jnp.bfloat16
F32 = jnp.float32
I32 = jnp.int32
MESH = pl.DeviceIdType.MESH


def iota(shape, dim):
    return lax.broadcasted_iota(I32, shape, dim)


def dot(a, b):
    return jnp.dot(a, b, preferred_element_type=F32)


def dot_nt(a, b):
    return lax.dot_general(a, b, (((1,), (1,)), ((), ())), preferred_element_type=F32)


def one_hot(condition):
    return jnp.where(condition, 1.0, 0.0).astype(BF)


def position_of(row, half, n_seq):
    run = half // n_seq
    block = (row % half) // run
    groups = n_seq // GROUP
    residue = (block % groups) * GROUP + block // groups
    return (row // half) * half + (row % run) * n_seq + residue


def row_of(position, half, n_seq):
    run = half // n_seq
    within = position % half
    residue = within % n_seq
    block = (residue % GROUP) * (n_seq // GROUP) + residue // GROUP
    return (position // half) * half + block * run + within // n_seq


def layer_norm(values, axis):
    mean = jnp.mean(values, axis, keepdims=True)
    centred = values - mean
    var = jnp.mean(centred * centred, axis, keepdims=True)
    return centred * lax.rsqrt(var + 1e-05)


def pieces(value):
    first = value.astype(BF).astype(F32)
    second = (value - first).astype(BF).astype(F32)
    return first, second, value - first - second


def soft_units(units):
    def score(unit):
        keys, query, head, _, _ = unit
        q = query()
        width = q.shape[1]
        zero = jnp.zeros(q.shape, BF)
        flag = one_hot(iota((32, width), 0) == 0)
        return dot(keys(), jnp.concatenate(([q, zero] if head == 0 else [zero, q]) + [flag], 0))

    def finish(unit, top, weights):
        values, sink = unit[3], unit[4]
        v = values()
        both = jnp.concatenate([v, jnp.ones((TAIL, v.shape[1]), BF)], 0)
        result = dot(both, weights)
        size = v.shape[0]
        total = result[size : size + 1]
        sink(result[:size] * (1.0 / total), top + jnp.log2(total))

    scores, held = score(units[0]), None
    for index, unit in enumerate(units):
        later = score(units[index + 1]) if index + 1 < len(units) else None
        top = jnp.max(scores, 0, keepdims=True)
        weights = jnp.exp2(scores - top).astype(BF)
        if held is not None:
            finish(*held)
        held, scores = (unit, top, weights), later
    finish(*held)


def layer_kernel(
    dims, counts_hbm, route_hbm, tiles_hbm, w_qkv_ref, w_out_ref, out_ref,
    counts_ref, route_ref, tiles_ref, placed, normed_ref, w_qkv, w_out, wq_t, wv_t, wk, wo_t, outgoing, arrived, meta_out, meta_in,
    q_t, keys, v_t, att, near, near_log,
    mid_q, mid_k, mid_v, mid_out, mid_back, wide_qv, wide_k, wide_qv_in, wide_k_in, wide_out, wide_back,
    load_sem, d_send, d_recv, p_send, p_recv, mf_send, mf_recv, wf_send, wf_recv, mb_send, mb_recv,
    wb_send, wb_recv, own_sem,
):
    n_slide, n_seq, most, stride = dims
    owners = n_slide * n_seq
    rows, width = tiles_ref.shape
    half = rows // 2
    run = half // n_seq
    taken = 2 * run
    size = width // HEADS
    duo = 2 * size
    middle_width = width // 2
    factor = math.log2(math.e) / math.sqrt(size)
    slide, seq = lax.axis_index("slide"), lax.axis_index("seq")
    member = seq % GROUP
    group = seq // GROUP
    groups = n_seq // GROUP
    base = seq - member

    def device_at(k):
        return ((slide + k // n_seq) % n_slide, (seq + k % n_seq) % n_seq)

    barrier = pltpu.get_barrier_semaphore()

    def greet(k, carry):
        pl.semaphore_signal(barrier, inc=1, device_id=device_at(k), device_id_type=MESH)
        return carry

    lax.fori_loop(1, owners, greet, 0)
    load_route = pltpu.make_async_copy(route_hbm, route_ref, load_sem.at[2])
    load_tiles = pltpu.make_async_copy(tiles_hbm, tiles_ref, load_sem.at[3])
    load_counts = pltpu.make_async_copy(counts_hbm, counts_ref, load_sem.at[4])
    load_route.start()
    load_tiles.start()
    load_counts.start()
    load_qkv = pltpu.make_async_copy(w_qkv_ref, w_qkv, load_sem.at[0])
    load_out = pltpu.make_async_copy(w_out_ref, w_out, load_sem.at[1])
    load_qkv.start()
    load_out.start()

    if stride > most:
        arrived[:, most:, :] = jnp.zeros((owners, stride - most, width), BF)
    upper = one_hot(iota((rows, rows), 0) <= iota((rows, rows), 1))
    load_route.wait()
    route = route_ref[...]
    owner = route // rows
    offset = ((owner // n_seq - slide + n_slide) % n_slide) * n_seq
    offset = offset + (owner % n_seq - seq + n_seq) % n_seq
    mine = iota((owners, rows), 0) == offset
    counted = dot(one_hot(mine), upper)
    rank = jnp.sum(jnp.where(mine, counted, 0.0), 0, keepdims=True).astype(I32) - 1
    slot = offset * stride + rank
    local = row_of(route % rows, half, n_seq)
    kind = iota((16, rows), 0)
    digits = jnp.where(
        kind == 0, local // 32, jnp.where(kind == 1, local % 32, jnp.where(kind == 2, 1, 0))
    ).astype(F32).astype(BF)

    def dispatch_copy(k):
        return pltpu.make_async_remote_copy(
            src_ref=outgoing.at[k, pl.ds(0, most)], dst_ref=arrived.at[k, pl.ds(0, most)],
            send_sem=d_send.at[k], recv_sem=d_recv.at[k], device_id=device_at(k), device_id_type=MESH,
        )

    per_row = LANES // stride

    def place_copy(k):
        return pltpu.make_async_remote_copy(
            src_ref=meta_out.at[k // per_row], dst_ref=meta_in.at[k],
            send_sem=p_send.at[k], recv_sem=p_recv.at[k], device_id=device_at(k), device_id_type=MESH,
        )

    def start_dispatch(k, carry):
        place_copy(k).start()
        dispatch_copy(k).start()
        return carry

    load_tiles.wait()
    load_counts.wait()
    chunk = 2 * LANES
    blocks = chunk // stride
    steps = owners // blocks

    def make_chunk(c):
        move = one_hot(iota((chunk, rows), 0) + c * chunk == slot)
        sent = dot_nt(digits, move)
        place = sent[0:1] * 32.0 + sent[1:2] + (1.0 - sent[2:3]) * (2.0 * rows)
        for i in range(2):
            meta_out[2 * c + i] = place[:, i * LANES : (i + 1) * LANES]
        moved = dot(move, tiles_ref[...]).astype(BF)
        outgoing[pl.ds(c * blocks, blocks)] = moved.reshape(blocks, stride, width)

    make_chunk(0)
    arrived[0] = outgoing[0]
    meta_in[0] = meta_out[0]
    pl.semaphore_wait(barrier, owners - 1)
    lax.fori_loop(1, blocks, start_dispatch, 0)

    def send_chunk(c, carry):
        make_chunk(c)
        return lax.fori_loop(c * blocks, (c + 1) * blocks, start_dispatch, carry)

    lax.fori_loop(1, steps, send_chunk, 0)
    placed[...] = jnp.zeros((rows, width), BF)
    normed_ref[...] = jnp.zeros((rows, width), BF)

    load_qkv.wait()
    load_out.wait()
    feature = iota((width, width), 0)
    head = (feature % middle_width) // duo + GROUP * (feature // middle_width) + 2 * GROUP * ((feature % duo) // size)
    reorder = one_hot(head * size + feature % size == iota((width, width), 1))
    wq_t[...] = dot_nt(reorder, w_qkv[:, :width]).astype(BF)
    wv_t[...] = dot_nt(reorder, w_qkv[:, 2 * width :]).astype(BF)
    padded = HEADS // 2 * LANES
    column = iota((width, padded), 1)
    pair, lane = column // LANES, column % LANES
    source = (pair + 2 * GROUP * (lane // size)) * size + lane % size
    pick = one_hot((iota((width, padded), 0) == source) & (lane < duo))
    wk[...] = dot(w_qkv[:, width : 2 * width], pick).astype(BF)
    unit_matrix = one_hot(iota((width, width), 0) == iota((width, width), 1))
    wo_t[...] = dot_nt(unit_matrix, dot(reorder, w_out[...]).astype(BF)).astype(BF)

    def wait_dispatch(k, carry):
        place_copy(k).wait_recv()
        dispatch_copy(k).wait_recv()
        return carry

    def places(first, count):
        parts = []
        for i in range(count * 2):
            tile = (2 * first + i) * per_row
            part = meta_in[tile]
            for b in range(1, per_row):
                part = jnp.where(iota((1, LANES), 1) // stride == b, meta_in[tile + b], part)
            parts.append(part)
        return jnp.concatenate(parts, 1).astype(I32)

    def arrivals(first, count):
        return arrived[pl.ds(first * blocks, count * blocks)].reshape(count * chunk, width)

    def spread(place, block):
        return dot(one_hot(iota((rows, place.shape[1]), 0) == place), block).astype(BF)

    def place_rows(first, count):
        placed[...] += spread(position_of(places(first, count), half, n_seq), arrivals(first, count))

    def place_norms(first, count):
        lax.fori_loop(jnp.maximum(1, first * blocks), (first + count) * blocks, wait_dispatch, 0)
        normed_ref[...] += spread(
            places(first, count), layer_norm(arrivals(first, count).astype(F32), 1).astype(BF)
        )

    def place_two(g, carry):
        place_norms(2 * g, 2)
        place_rows(2 * g, 2)
        return carry

    def place_one(g, carry):
        place_norms(g, 1)
        return carry

    lax.fori_loop(0, steps // 2 - 1, place_two, 0)
    lax.fori_loop(steps - 2, steps, place_one, 0)

    limit = counts_ref[slide] - seq * rows

    def pair_at(turn):
        return (group + turn) % 2

    def project(turn):
        j = pair_at(turn)
        part = pl.ds(pl.multiple_of(j * middle_width, middle_width), middle_width)
        columns = pl.ds(pl.multiple_of(j * GROUP * LANES, GROUP * LANES), GROUP * LANES)

        def one_segment(seg, carry):
            normed = normed_ref[pl.ds(seg * half, half), :]
            q = (dot_nt(wq_t[part, :], normed) * factor).astype(BF)
            v = dot_nt(wv_t[part, :], normed).astype(BF)
            for cb in range(GROUP):
                q_t[cb, seg, part, :] = q[:, cb * LANES : (cb + 1) * LANES]
                v_t[cb, seg, part, :] = v[:, cb * LANES : (cb + 1) * LANES]
            at = iota((half, GROUP * LANES), 0) + seg * half
            valid = position_of(at, half, n_seq) < limit
            lane = iota((half, GROUP * LANES), 1) % LANES
            bias = jnp.where((lane == duo) & jnp.logical_not(valid), -1e30, 0.0)
            k = (dot(normed, wk[:, columns]) + bias).astype(BF)
            for o in range(GROUP):
                keys[j, o, seg] = k[:, o * LANES : (o + 1) * LANES]
            return carry

        for seg in range(2):
            one_segment(seg, 0)
            if turn == 0:
                start_mid(0, seg)

    def mid_sources(o, j, seg):
        part = pl.ds(pl.multiple_of(j * middle_width + o * duo, duo), duo)
        return (
            q_t.at[o, seg, part, :],
            keys.at[j, o, seg, pl.ds(pl.multiple_of(o * LANES, LANES), LANES), :],
            v_t.at[o, seg, part, :],
        )

    def mid_copies(k, turn, seg):
        to = (member + k) % GROUP
        return [
            pltpu.make_async_remote_copy(
                src_ref=src, dst_ref=dst.at[turn, k, seg], send_sem=mf_send.at[turn, k, seg, i],
                recv_sem=mf_recv.at[turn, k, seg, i], device_id=(slide, base + to), device_id_type=MESH,
            )
            for i, (src, dst) in enumerate(zip(mid_sources(to, pair_at(turn), seg), (mid_q, mid_k, mid_v)))
        ]

    def start_mid(turn, seg):
        for k in range(1, GROUP):
            for copy in mid_copies(k, turn, seg):
                copy.start()

    project(0)
    project(1)

    for r in range(n_seq):
        o, j, g = r % GROUP, (r // GROUP) % 2, r // GROUP
        start = j * middle_width + o * duo
        for index, ref in enumerate((q_t, v_t)):
            wide_qv[r, index] = jnp.concatenate(
                [ref[o, seg, start : start + duo, g * run : (g + 1) * run] for seg in range(2)], 1
            )
        for seg in range(2):
            first = o * LANES + g * run
            wide_k[r, seg * run : (seg + 1) * run] = keys[j, o, seg, first : first + run]

    def seq_at(k):
        return (group + k // GROUP) % groups * GROUP + (member + k % GROUP) % GROUP

    def seq_back(k):
        return (group - k // GROUP + groups) % groups * GROUP + (member - k % GROUP + GROUP) % GROUP

    def wide_copies(k):
        to = seq_at(k)
        return [
            pltpu.make_async_remote_copy(
                src_ref=src.at[to], dst_ref=dst.at[k], send_sem=wf_send.at[k, i], recv_sem=wf_recv.at[k, i],
                device_id=(slide, to), device_id_type=MESH,
            )
            for i, (src, dst) in enumerate(((wide_qv, wide_qv_in), (wide_k, wide_k_in)))
        ]

    for k in range(GROUP, n_seq):
        for copy in wide_copies(k):
            copy.start()
    own = [
        pltpu.make_async_copy(src, dst.at[turn, 0, seg], own_sem.at[5 + 6 * turn + 3 * seg + i])
        for turn in range(2)
        for seg in range(2)
        for i, (src, dst) in enumerate(zip(mid_sources(member, pair_at(turn), seg), (mid_q, mid_k, mid_v)))
    ]
    for copy in own:
        copy.start()

    def near_owner(o, carry):
        @pl.when(o == 2)
        def _():
            for seg in range(2):
                start_mid(1, seg)

        units = []
        for j in range(2):
            for seg in range(2):
                for t in range(2):
                    part = pl.ds(pl.multiple_of(o * duo + (j * middle_width + t * size), TAIL), size)

                    def wide_row(ref, seg=seg, part=part):
                        return jnp.concatenate([ref[cb, seg, part, :] for cb in range(GROUP)], 1)

                    def sink(result, log, j=j, seg=seg, t=t, part=part):
                        for cb in range(GROUP):
                            cut = slice(cb * LANES, (cb + 1) * LANES)
                            att[seg, cb, part, :] = result[:, cut].astype(BF)
                            near[o, j, seg, t, cb] = result[:, cut]
                            near_log[o, j, seg, t, cb] = log[:, cut]

                    units.append((
                        lambda j=j, seg=seg: keys[j, o, seg],
                        lambda wide_row=wide_row: wide_row(q_t),
                        t,
                        lambda wide_row=wide_row: wide_row(v_t),
                        sink,
                    ))
        soft_units(units)
        return carry

    lax.fori_loop(0, GROUP, near_owner, 0)

    def log_tile(logs, lanes):
        tile = jnp.zeros((TAIL, lanes), F32)
        where = iota((TAIL, lanes), 0)
        for index, piece in enumerate(pieces(logs[0]) + pieces(logs[1])):
            tile = jnp.where(where == index, piece, tile)
        return tile.astype(BF)

    for copy in own:
        copy.wait()

    def mid_return(k, turn, seg):
        return pltpu.make_async_remote_copy(
            src_ref=mid_out.at[turn, k, seg], dst_ref=mid_back.at[member, pair_at(turn), seg],
            send_sem=mb_send.at[turn, k, seg], recv_sem=mb_recv.at[turn, k, seg],
            device_id=(slide, base + (member - k + GROUP) % GROUP), device_id_type=MESH,
        )

    def wide_return(k):
        return pltpu.make_async_remote_copy(
            src_ref=wide_out.at[k], dst_ref=wide_back.at[seq], send_sem=wb_send.at[k], recv_sem=wb_recv.at[k],
            device_id=(slide, seq_back(k)), device_id_type=MESH,
        )

    def middle(turn):
        slots = (1, 2, 3, 0)
        units = []
        for seg in range(2):
            logs = []
            for t in range(2):
                cut = slice(t * size, (t + 1) * size)

                def sink(result, log, t=t, cut=cut, seg=seg, logs=logs):
                    logs.append(log)
                    for index, k in enumerate(slots):
                        lanes = slice(index * LANES, (index + 1) * LANES)
                        mid_out[turn, k, seg, cut] = result[:, lanes].astype(BF)
                        if t == 1:
                            mid_out[turn, k, seg, duo:] = log_tile([one[:, lanes] for one in logs], LANES)
                            if k:
                                mid_return(k, turn, seg).start()

                units.append((
                    lambda: mid_k[turn].reshape(rows, LANES),
                    lambda seg=seg, cut=cut: jnp.concatenate([mid_q[turn, k, seg, cut] for k in slots], 1),
                    t,
                    lambda cut=cut: jnp.concatenate(
                        [mid_v[turn, k, seg, cut] for k in range(GROUP) for seg in range(2)], 1
                    ),
                    sink,
                ))
        return units

    def widest():
        order = [k % n_seq for k in range(1, n_seq + 1)]
        count = n_seq // 2
        units = []
        for part in range(2):
            slots = order[part * count : (part + 1) * count]
            logs = []
            for t in range(2):
                cut = slice(t * size, (t + 1) * size)

                def sink(result, log, t=t, slots=slots, cut=cut, logs=logs):
                    logs.append(log)
                    for index, k in enumerate(slots):
                        lanes = slice(index * taken, (index + 1) * taken)
                        wide_out[k, cut] = result[:, lanes].astype(BF)
                        if t == 1:
                            wide_out[k, duo:] = log_tile([one[:, lanes] for one in logs], taken)
                            if k:
                                wide_return(k).start()

                units.append((
                    lambda: wide_k_in[...].reshape(n_seq * taken, LANES),
                    lambda slots=slots, cut=cut: jnp.concatenate([wide_qv_in[k, 0, cut] for k in slots], 1),
                    t,
                    lambda cut=cut: jnp.concatenate([wide_qv_in[k, 1, cut] for k in range(n_seq)], 1),
                    sink,
                ))
        return units

    for k in range(1, GROUP):
        for seg in range(2):
            for copy in mid_copies(k, 0, seg):
                copy.wait_recv()
    for k in range(GROUP):
        for index, ref in enumerate((mid_q, mid_v)):
            first, second = ref[0, k, 0], ref[0, k, 1]
            own_part = None
            for g in range(groups):
                lanes = slice(g * run, (g + 1) * run)
                part = jnp.concatenate([first[:, lanes], second[:, lanes]], 1)
                own_part = part if g == 0 else jnp.where(group == g, part, own_part)
            wide_qv_in[k, index] = own_part
        for seg in range(2):
            wide_k_in[k, seg * run : (seg + 1) * run] = mid_k[0, k, seg, pl.ds(pl.multiple_of(group * run, run), run)]
    soft_units(middle(0))
    for k in range(GROUP, n_seq):
        for copy in wide_copies(k):
            copy.wait_recv()
    soft_units(widest())
    own_wide = pltpu.make_async_copy(wide_out.at[0], wide_back.at[seq], own_sem.at[0])
    own_wide.start()
    place_rows(steps - 2, 2)
    for k in range(1, GROUP):
        for seg in range(2):
            for copy in mid_copies(k, 1, seg):
                copy.wait_recv()
    soft_units(middle(1))
    own_mid = [
        pltpu.make_async_copy(
            mid_out.at[turn, 0, seg], mid_back.at[member, pair_at(turn), seg], own_sem.at[1 + 2 * turn + seg]
        )
        for turn in range(2)
        for seg in range(2)
    ]
    for copy in own_mid:
        copy.start()

    unsort = one_hot(row_of(iota((half, half), 0), half, n_seq) == iota((half, half), 1))

    own_wide.wait()
    for copy in own_mid:
        copy.wait()
    for k in range(1, n_seq):
        wide_return(k).wait_recv()

    def log_of(tile, t):
        return tile[3 * t : 3 * t + 1] + tile[3 * t + 1 : 3 * t + 2] + tile[3 * t + 2 : 3 * t + 3]

    def embed(value, g, fill):
        before = [jnp.full((value.shape[0], g * run), fill, F32)] if g else []
        after = LANES - (g + 1) * run
        behind = [jnp.full((value.shape[0], after), fill, F32)] if after else []
        return jnp.concatenate(before + [value] + behind, 1)

    def merge_owner(o, seg):
        for j in range(2):
            for t in range(2):
                first = (GROUP * j + 2 * GROUP * t) % n_seq
                wide = wide_back[first + o].astype(F32)
                cut = slice(t * size, (t + 1) * size)
                rows_of = pl.ds(o * duo + (j * middle_width + t * size), size)
                lanes = slice(seg * run, (seg + 1) * run)
                wide_o = embed(wide[cut, lanes], first // GROUP, 0.0)
                log_w = embed(log_of(wide[duo:, lanes], t), first // GROUP, -3e30)
                mid = mid_back[o, j, seg].astype(F32)
                log_m = log_of(mid[duo:], t)
                log_n = near_log[o, j, seg, t, o]
                top = jnp.maximum(jnp.maximum(log_n, log_m), log_w)
                share_n, share_m, share_w = jnp.exp2(log_n - top), jnp.exp2(log_m - top), jnp.exp2(log_w - top)
                scale = 1.0 / (share_n + share_m + share_w)
                merged = (
                    near[o, j, seg, t, o] * (share_n * scale)
                    + mid[cut] * (share_m * scale)
                    + wide_o * (share_w * scale)
                )
                att[seg, o, rows_of, :] = merged.astype(BF)


    def store(seg):
        part = pl.ds(seg * half, half)
        return pltpu.make_async_copy(tiles_ref.at[part], out_ref.at[part], load_sem.at[seg])

    def finish_segment(seg, carry):
        part = pl.ds(seg * half, half)
        attended = jnp.concatenate([att[seg, cb] for cb in range(GROUP)], 1)
        normed = layer_norm(dot(wo_t[...], attended), 0).astype(BF)
        value = dot_nt(unsort, normed) + placed[part, :].astype(F32)
        position = iota((half, width), 0) + seg * half
        tiles_ref[part, :] = jnp.where(position < limit, value, 0.0).astype(BF)
        store(seg).start()
        return carry

    for seg in range(2):
        for k in range(1, GROUP):
            for turn in range(2):
                mid_return(k, turn, seg).wait_recv()
        for o in range(GROUP):
            merge_owner(o, seg)
        finish_segment(seg, 0)

    def drain(k, carry):
        place_copy(k).wait_send()
        dispatch_copy(k).wait_send()
        return carry

    lax.fori_loop(1, owners, drain, 0)
    for k in range(1, n_seq):
        if k >= GROUP:
            for copy in wide_copies(k):
                copy.wait_send()
        wide_return(k).wait_send()
    for k in range(1, GROUP):
        for turn in range(2):
            for seg in range(2):
                for copy in mid_copies(k, turn, seg):
                    copy.wait_send()
                mid_return(k, turn, seg).wait_send()
    for seg in range(2):
        store(seg).wait()


def body(tiles, route, counts, w_qkv, w_out):
    rows, width = tiles.shape
    n_slide = lax.axis_size("slide")
    n_seq = lax.axis_size("seq")
    owners = n_slide * n_seq
    most = -(-(3 * rows // (2 * owners)) // 16) * 16
    stride = 1 << (most - 1).bit_length()
    half = rows // 2
    taken = rows // n_seq
    size = width // HEADS
    duo = 2 * size
    back = duo + TAIL
    dma = pltpu.SemaphoreType.DMA

    def buffer(*shape, dtype=BF):
        return pltpu.VMEM(shape, dtype)

    return pl.pallas_call(
        functools.partial(layer_kernel, (n_slide, n_seq, most, stride)),
        out_shape=jax.ShapeDtypeStruct((rows, width), BF),
        in_specs=[
            pl.BlockSpec(memory_space=pl.ANY),
        ] * 5,
        out_specs=pl.BlockSpec(memory_space=pl.ANY),
        scratch_shapes=[
            pltpu.SMEM((n_slide,), I32),
            buffer(1, rows, dtype=I32),
            buffer(rows, width),
            buffer(rows, width),
            buffer(rows, width),
            buffer(width, 3 * width),
            buffer(width, width),
            buffer(width, width),
            buffer(width, width),
            buffer(width, HEADS // 2 * LANES),
            buffer(width, width),
            buffer(owners, stride, width),
            buffer(owners, stride, width),
            buffer(owners * stride // LANES, 1, LANES, dtype=F32),
            buffer(owners, 1, LANES, dtype=F32),
            buffer(GROUP, 2, width, LANES),
            buffer(2, GROUP, 2, half, LANES),
            buffer(GROUP, 2, width, LANES),
            buffer(2, GROUP, width, LANES),
            buffer(GROUP, 2, 2, 2, GROUP, size, LANES, dtype=F32),
            buffer(GROUP, 2, 2, 2, GROUP, 1, LANES, dtype=F32),
            buffer(2, GROUP, 2, duo, LANES),
            buffer(2, GROUP, 2, LANES, LANES),
            buffer(2, GROUP, 2, duo, LANES),
            buffer(2, GROUP, 2, back, LANES),
            buffer(GROUP, 2, 2, back, LANES),
            buffer(n_seq, 2, duo, taken),
            buffer(n_seq, taken, LANES),
            buffer(n_seq, 2, duo, taken),
            buffer(n_seq, taken, LANES),
            buffer(n_seq, back, taken),
            buffer(n_seq, back, taken),
            dma((5,)),
            dma((owners,)), dma((owners,)), dma((owners,)), dma((owners,)),
            dma((2, GROUP, 2, 3)), dma((2, GROUP, 2, 3)), dma((n_seq, 2)), dma((n_seq, 2)),
            dma((2, GROUP, 2)), dma((2, GROUP, 2)), dma((n_seq,)), dma((n_seq,)),
            dma((17,)),
        ],
        compiler_params=pltpu.CompilerParams(
            collective_id=0, has_side_effects=True, vmem_limit_bytes=58 << 20
        ),
        name="layer",
    )(counts, route.reshape(1, rows), tiles, w_qkv, w_out)


def solution(mesh):
    return jax.shard_map(
        body,
        mesh=mesh,
        in_specs=(P(("slide", "seq"), None), P(("slide", "seq")), P(), P(), P()),
        out_specs=P(("slide", "seq"), None),
        check_vma=False,
    )
```
